32 devices in a mesh: dp: 8 (over z, core), expert: 4 (over y, x).
Axes of the slice: x: 2, y: 2, z: 4, core: 2. Of those that a mesh axis runs over, the one named last changes fastest.
Arguments:
- tokens: bfloat16 [4096, 2048], P(('dp', 'expert')), may hold values from -6 to 6
- expert_ids: int32 [4096, 8], P(('dp', 'expert')), may hold values from 0 to 127, as said below
- gate_probs: float32 [4096, 8], P(('dp', 'expert')), may hold values from 0.1 to 1
- cotangent: bfloat16 [4096, 2048], P(('dp', 'expert')), may hold values from -1.5 to 1.5
- expert_weights: bfloat16 [2048, 4, 3, 768], P(None, 'expert'), may hold values from -0.21875 to 0.21875
Outputs:
- mixed: bfloat16 [4096, 2048], P(('dp', 'expert'))
- grad_tokens: bfloat16 [4096, 2048], P(('dp', 'expert'))
- grad_gates: float32 [4096, 8], P(('dp', 'expert'))
- grad_weights: bfloat16 [2048, 4, 3, 768], P('dp', 'expert')
The draws below stay inside these ranges and needn't reach their ends.
Inputs may be any that keep to these rules, and one draw needn't show every extreme that they name: `expert_ids`: each row names 8 different experts. In the rows of one device every expert below 4 is named by 1 to 24 rows, and for every index of dp some such expert is named by exactly 24 rows of each device of that index.
All inputs are finite; a program needn't handle non-finite values.
Results may differ from the reference program's by a relative error of at most 0.0058.
Values may be sent and summed in bfloat16 or wider, within the bound.
No kernel may reach another device: no remote copies, remote signals or barrier semaphores. Data moves between devices by JAX's collectives and lax.ppermute only.
A program may use at most 128 MiB of HBM per device.

```python
import math
import jax
import jax.numpy as jnp
from jax import lax

D = 2048
FF = 768
EXPERTS = 128
TOPK = 8
TOK_DEV = 128
HELD = 4
CAP = 24
TOKENS = 4096
N_DP = 8


def draw_expert_ids(key, part):
    blocks = TOKENS // TOK_DEV
    groups = blocks // HELD
    key_hottest, key_counts, key_filler, key_order, key_rolls = jax.random.split(key, 5)
    hottest = jax.random.randint(key_hottest, (groups,), 0, HELD)
    counts = jax.random.randint(key_counts, (groups, HELD, HELD), 1, CAP // 2 + 1)
    is_hottest = jnp.arange(HELD)[None, None, :] == hottest[:, None, None]
    counts = jnp.where(is_hottest, CAP, counts).reshape(blocks, HELD)
    row_index = jnp.arange(TOK_DEV)[:, None]
    slot_index = jnp.arange(TOPK)[None, :]
    position = slot_index * TOK_DEV + row_index
    bounds = jnp.cumsum(counts, axis=1)
    owner = jnp.sum((position[None, :, :, None] >= bounds[:, None, None, :]).astype(jnp.int32), axis=-1)
    totals = bounds[:, -1]
    offsets = jax.random.randint(key_filler, (blocks, TOK_DEV, 1), 0, EXPERTS - HELD)
    filler = HELD + (slot_index[None, :, :] + offsets) % (EXPERTS - HELD)
    chosen = jnp.where(position[None, :, :] < totals[:, None, None], owner, filler)
    order_keys = jax.random.split(key_order, blocks)
    orders = jax.vmap(lambda subkey: jax.random.permutation(subkey, TOK_DEV))(order_keys)
    chosen = jnp.take_along_axis(chosen, orders[:, :, None], axis=1)
    rolls = jax.random.randint(key_rolls, (blocks, TOK_DEV, 1), 0, TOPK)
    columns = (slot_index[None, :, :] + rolls) % TOPK
    chosen = jnp.take_along_axis(chosen, columns, axis=2)
    return chosen.reshape(TOKENS, TOPK).astype(jnp.int32)


def levels(rng, dims, cuts, least, largest):
    level = 1.0
    for dim, parts in cuts:
        heights = jax.random.uniform(jax.random.fold_in(jax.random.fold_in(rng, 6), dim), (parts,), jnp.float32, least / len(cuts), largest / len(cuts))
        level = level * jnp.repeat(jnp.exp(heights), dims[dim] // parts).reshape((-1,) + (1,) * (len(dims) - 1 - dim))
    return level


def normal_values(key, dims, scale, reach, cuts=(), held_as=jnp.bfloat16):
    gain = levels(key, dims, cuts, -0.22, 0.18) if cuts else 1.0
    result = jax.random.normal(key, dims, jnp.float32) * scale * gain
    return jnp.minimum(jnp.maximum(result, -reach), reach).astype(held_as)


def setup_inputs(seed: int = 0) -> dict:
    key_list = jax.random.split(jax.random.key(seed), 6)
    return {
        "tokens": normal_values(key_list[0], (TOKENS, D), 1.0, 6.0, ((0, 32),)),
        "expert_ids": draw_expert_ids(jax.random.fold_in(key_list[5], 71), 0),
        "gate_probs": jnp.clip(jnp.exp(math.log(1.0) - 2.3025851 * jax.random.uniform(key_list[2], (TOKENS, TOPK), jnp.float32) ** levels(key_list[2], (TOKENS, TOPK), ((0, 32),), -0.2, 0.2)), 0.1, 1.0),
        "cotangent": normal_values(key_list[3], (TOKENS, D), 0.25, 1.5, ((0, 32),)),
        "expert_weights": normal_values(key_list[4], (D, HELD, 3, FF), FF ** -0.5, 0.21875, ((1, 4),)),
    }


def expert_rows(x_rows, dy_rows, weights):
    w_gate = weights[:, 0, :]
    w_up = weights[:, 1, :]
    w_down = weights[:, 2, :]
    contract_last = (((1,), (1,)), ((), ()))
    gate_proj = jnp.dot(x_rows, w_gate, preferred_element_type=jnp.float32)
    up_proj = jnp.dot(x_rows, w_up, preferred_element_type=jnp.float32)
    sigmoid_gate = jax.nn.sigmoid(gate_proj)
    silu_gate = gate_proj * sigmoid_gate
    hidden = (silu_gate * up_proj).astype(jnp.bfloat16)
    expert_out = lax.dot_general(hidden, w_down, contract_last, preferred_element_type=jnp.float32).astype(jnp.bfloat16)
    hidden_grad = jnp.dot(dy_rows, w_down, preferred_element_type=jnp.float32)
    gate_grad = (hidden_grad * up_proj * sigmoid_gate * (1.0 + gate_proj * (1.0 - sigmoid_gate))).astype(jnp.bfloat16)
    up_grad = (hidden_grad * silu_gate).astype(jnp.bfloat16)
    token_part = (lax.dot_general(gate_grad, w_gate, contract_last, preferred_element_type=jnp.float32)
                  + lax.dot_general(up_grad, w_up, contract_last, preferred_element_type=jnp.float32)).astype(jnp.bfloat16)
    return expert_out, token_part, hidden, gate_grad, up_grad


def reference(tokens, expert_ids, gate_probs, cotangent, expert_weights):
    assign_total = TOKENS * TOPK
    most_rows = N_DP * HELD * CAP
    flat_ids = expert_ids.reshape(-1)
    flat_probs = gate_probs.reshape(-1)
    token_of = (jnp.arange(assign_total) // TOPK).astype(jnp.int32)
    assign_index = jnp.arange(assign_total).astype(jnp.int32)
    row_index = jnp.arange(most_rows).astype(jnp.int32)
    contract_first = (((0,), (0,)), ((), ()))

    def per_expert(state_in, expert):
        mixed_sum, token_sum, gate_sum = state_in
        chosen = flat_ids == expert
        rank_in = jnp.cumsum(chosen.astype(jnp.int32)) - 1
        target = jnp.where(chosen, rank_in, most_rows).astype(jnp.int32)
        picked = jnp.zeros((most_rows,), jnp.int32).at[target].set(assign_index, mode="drop")
        is_valid = row_index < jnp.sum(chosen.astype(jnp.int32))
        row_tokens = token_of[picked]
        row_probs = jnp.where(is_valid, flat_probs[picked], jnp.zeros((), jnp.float32))
        x_rows = jnp.where(is_valid[:, None], tokens[row_tokens], jnp.zeros((), jnp.bfloat16))
        dy_rows = (row_probs[:, None] * cotangent[row_tokens].astype(jnp.float32)).astype(jnp.bfloat16)
        weights = lax.dynamic_index_in_dim(expert_weights, expert, 1, keepdims=False)
        expert_out, token_part, hidden, gate_grad, up_grad = expert_rows(x_rows, dy_rows, weights)
        out_float = expert_out.astype(jnp.float32)
        mixed_sum = mixed_sum.at[row_tokens].add(row_probs[:, None] * out_float)
        token_sum = token_sum.at[row_tokens].add(
            jnp.where(is_valid[:, None], token_part.astype(jnp.float32), jnp.zeros((), jnp.float32)))
        inner_prod = jnp.sum(out_float * cotangent[row_tokens].astype(jnp.float32), axis=1)
        gate_sum = gate_sum.at[picked].add(jnp.where(is_valid, inner_prod, jnp.zeros((), jnp.float32)))
        weight_grad = jnp.stack([
            lax.dot_general(x_rows, gate_grad, contract_first, preferred_element_type=jnp.float32),
            lax.dot_general(x_rows, up_grad, contract_first, preferred_element_type=jnp.float32),
            lax.dot_general(dy_rows, hidden, contract_first, preferred_element_type=jnp.float32)], axis=1)
        return (mixed_sum, token_sum, gate_sum), weight_grad

    initial = (jnp.zeros((TOKENS, D), jnp.float32), jnp.zeros((TOKENS, D), jnp.float32),
               jnp.zeros((assign_total,), jnp.float32))
    final_state, stacked = lax.scan(per_expert, initial, jnp.arange(HELD).astype(jnp.int32))
    mixed_sum, token_sum, gate_sum = final_state
    grad_weights = jnp.transpose(stacked, (1, 0, 2, 3)).astype(jnp.bfloat16)
    return (mixed_sum.astype(jnp.bfloat16), token_sum.astype(jnp.bfloat16),
            gate_sum.reshape(TOKENS, TOPK), grad_weights)
```

```python
import functools

import jax
import jax.numpy as jnp
from jax import lax
from jax.experimental import pallas as pl
from jax.experimental.pallas import tpu as pltpu
from jax.sharding import PartitionSpec as P

CAP = 24
CORES = 2
F32 = jnp.float32
BF16 = jnp.bfloat16
VMEM = pl.BlockSpec(memory_space=pltpu.VMEM)
SMEM = pl.BlockSpec(memory_space=pltpu.SMEM)
NT = (((1,), (1,)), ((), ()))
TN = (((0,), (0,)), ((), ()))


def shape_of(dims, dtype=BF16):
    return jax.ShapeDtypeStruct(dims, dtype)


def cost(flops, moved):
    return pl.CostEstimate(flops=int(flops), bytes_accessed=int(moved), transcendentals=0)


def slot_map(ids, probs, me, experts):
    tokens = ids.shape[1]
    before = (
        lax.broadcasted_iota(jnp.int32, (tokens, tokens), 0)
        < lax.broadcasted_iota(jnp.int32, (tokens, tokens), 1)
    ).astype(BF16)
    named = []
    weight = []
    for m in range(experts):
        hit = ids == jnp.bitwise_xor(me, m)
        named.append(jnp.sum(hit.astype(F32), axis=0, keepdims=True))
        weight.append(jnp.sum(jnp.where(hit, probs, 0.0), axis=0, keepdims=True))
    mask = jnp.concatenate(named, axis=0)
    pos = jnp.dot(mask.astype(BF16), before, preferred_element_type=F32)
    rank = lax.broadcasted_iota(jnp.int32, (CAP, tokens), 0).astype(F32)
    blocks = []
    slot_probs = []
    for m in range(experts):
        hot = jnp.where((rank == pos[m : m + 1]) & (mask[m : m + 1] > 0.5), 1.0, 0.0)
        blocks.append(hot)
        slot_probs.append(jnp.sum(hot * weight[m], axis=1, keepdims=True))
    return jnp.concatenate(blocks, axis=0), jnp.concatenate(slot_probs, axis=0)


def send_kernel(experts, where_ref, ids_ref, probs_ref, tok_ref, cot_ref, *outs):
    onehot, slot_probs = slot_map(ids_ref[...], probs_ref[...], where_ref[0], experts)
    pick = onehot.astype(BF16)
    x_rows = jnp.dot(pick, tok_ref[...], preferred_element_type=F32)
    dy_rows = slot_probs * jnp.dot(pick, cot_ref[...], preferred_element_type=F32)
    for m in range(experts):
        outs[m][...] = x_rows[m * CAP : (m + 1) * CAP].astype(BF16)
        outs[experts + m][...] = dy_rows[m * CAP : (m + 1) * CAP].astype(BF16)


def gather_rows(blocks):
    return jnp.concatenate([b[...].astype(F32) for b in blocks], axis=0).astype(BF16)


def emit_features(where_ref, rows_ref, outs, zs):
    part = outs[0].shape[1] // CORES
    z, c = where_ref[1], where_ref[2]
    for m in range(zs):
        chip = jnp.bitwise_xor(z, m) * CORES
        for j in range(CORES):
            start = (chip + jnp.bitwise_xor(c, j)) * part
            outs[m][:, j * part : (j + 1) * part] = rows_ref[
                :, pl.ds(pl.multiple_of(start, part), part)
            ]


def forward_kernel(experts, zs, where_ref, *refs):
    blocks, (wg, wu) = refs[:experts], refs[experts : experts + 2]
    gate_ref, up_ref, hid_ref = refs[experts + 2 : experts + 5]
    feats, rows = refs[experts + 5 : -1], refs[-1]

    @pl.when(pl.program_id(0) == 0)
    def _():
        rows[...] = gather_rows(blocks)
        emit_features(where_ref, rows, feats, zs)

    gate = jnp.dot(rows[...], wg[0], preferred_element_type=F32)
    up = jnp.dot(rows[...], wu[0], preferred_element_type=F32)
    gate_ref[...] = gate
    up_ref[...] = up
    hid_ref[...] = (gate * jax.nn.sigmoid(gate) * up).astype(BF16)


def backward_kernel(experts, zs, where_ref, *refs):
    blocks, (wd, gate_ref, up_ref) = refs[:experts], refs[experts : experts + 3]
    gg_ref, ug_ref = refs[experts + 3 : experts + 5]
    feats, rows = refs[experts + 5 : -1], refs[-1]

    @pl.when(pl.program_id(0) == 0)
    def _():
        rows[...] = gather_rows(blocks)
        emit_features(where_ref, rows, feats, zs)

    grad = jnp.dot(rows[...], wd[0], preferred_element_type=F32)
    gate, up = gate_ref[...], up_ref[...]
    s = jax.nn.sigmoid(gate)
    gg_ref[...] = (grad * up * s * (1.0 + gate * (1.0 - s))).astype(BF16)
    ug_ref[...] = (grad * (gate * s)).astype(BF16)


def output_kernel(experts, hid_ref, gg_ref, ug_ref, wg, wu, wd, *outs):
    out = lax.dot_general(hid_ref[...], wd[0], NT, preferred_element_type=F32)
    part = lax.dot_general(gg_ref[...], wg[0], NT, preferred_element_type=F32)
    part += lax.dot_general(ug_ref[...], wu[0], NT, preferred_element_type=F32)
    for m in range(experts):
        outs[m][0] = out[m * CAP : (m + 1) * CAP].astype(BF16)
        outs[m][1] = part[m * CAP : (m + 1) * CAP].astype(BF16)


def combine_kernel(experts, where_ref, ids_ref, probs_ref, cot_ref, *refs):
    blocks, (mixed_ref, gtok_ref, gates_ref) = refs[:experts], refs[experts:]
    ids = ids_ref[...]
    onehot, slot_probs = slot_map(ids, probs_ref[...], where_ref[0], experts)
    pick = onehot.astype(BF16)
    out = jnp.concatenate([b[0].astype(F32) for b in blocks], axis=0)
    part = jnp.concatenate([b[1].astype(F32) for b in blocks], axis=0)
    weighted = out * slot_probs
    high = weighted.astype(BF16)
    low = (weighted - high.astype(F32)).astype(BF16)
    mixed = lax.dot_general(pick, high, TN, preferred_element_type=F32)
    mixed += lax.dot_general(pick, low, TN, preferred_element_type=F32)
    mixed_ref[...] = mixed.astype(BF16)
    gtok = lax.dot_general(pick, part.astype(BF16), TN, preferred_element_type=F32)
    gtok_ref[...] = gtok.astype(BF16)
    cot_rows = jnp.dot(pick, cot_ref[...], preferred_element_type=F32)
    inner = jnp.sum(out * cot_rows, axis=1, keepdims=True)
    spread = onehot * inner
    gates = jnp.zeros(ids.shape, F32)
    for m in range(experts):
        value = jnp.sum(spread[m * CAP : (m + 1) * CAP], axis=0, keepdims=True)
        gates = jnp.where(ids == jnp.bitwise_xor(where_ref[0], m), value, gates)
    gates_ref[...] = gates


def weight_kernel(zs, picks, *refs):
    feats = refs[:zs]
    grads = refs[zs : zs + sum(picks)]
    own_ref, send_ref = refs[-2:]
    rows_f = jnp.concatenate([f[...].astype(F32) for f in feats], axis=0).astype(BF16)
    parts = []
    at = 0
    for n in picks:
        value = grads[at][...].astype(F32)
        for extra in grads[at + 1 : at + n]:
            value += extra[...].astype(F32)
        parts.append(value)
        at += n
    rows_g = jnp.concatenate(parts, axis=0).astype(BF16)
    total = lax.dot_general(rows_f, rows_g, TN, preferred_element_type=F32)
    half = total.shape[0] // CORES
    own_ref[...] = total[:half]
    send_ref[...] = total[half:].astype(BF16)


def final_kernel(*refs):
    out = refs[-1]
    n = (len(refs) - 1) // 2
    for j in range(n):
        out[j] = (refs[j][...] + refs[n + j][...].astype(F32)).astype(BF16)


def per_device(tokens, expert_ids, gate_probs, cotangent, expert_weights):
    tok_rows, width = tokens.shape
    experts = lax.axis_size("expert")
    groups = lax.axis_size("dp")
    zs = groups // CORES
    hidden = expert_weights.shape[3]
    rows = experts * CAP
    chip_width = width // zs
    me = lax.axis_index("expert")
    dp = lax.axis_index("dp")
    where = jnp.stack([me, dp // CORES, dp % CORES]).astype(jnp.int32)
    weights = jnp.transpose(expert_weights[:, 0], (1, 0, 2))
    ids, probs = expert_ids.T, gate_probs.T

    def swap_expert(block, m):
        if m == 0:
            return block
        return lax.ppermute(block, "expert", [(i, i ^ m) for i in range(experts)])

    def swap_z(block, m, only=None):
        pairs = []
        for z in range(zs):
            if only is None or z in only:
                pairs += [(z * CORES + c, (z ^ m) * CORES + c) for c in range(CORES)]
        return lax.ppermute(block, "dp", pairs)

    def spread_z(block):
        if zs != 4:
            return [[block]] + [[swap_z(block, m)] for m in range(1, zs)]
        far = swap_z(block, 2)
        near = swap_z(block, 1)
        middle = swap_z(block, 3, (1, 2))
        ends = swap_z(far, 1, (1, 2))
        return [[block], [near], [far], [middle, ends]]

    order = [m for m in range(experts - 1, 0, -1)]
    sent = pl.pallas_call(
        functools.partial(send_kernel, experts),
        out_shape=[shape_of((CAP, width))] * (2 * experts),
        in_specs=[SMEM] + [VMEM] * 4,
        out_specs=[VMEM] * (2 * experts),
        cost_estimate=cost(4 * rows * tok_rows * width, 8 * tok_rows * width),
        name="send",
    )(where, ids, probs, tokens, cotangent)
    x_blocks = {m: swap_expert(sent[m], m) for m in [0] + order}
    dy_blocks = {m: swap_expert(sent[experts + m], m) for m in [0] + order}
    x_blocks = [x_blocks[m] for m in range(experts)]
    dy_blocks = [dy_blocks[m] for m in range(experts)]

    chunk = 256 if hidden % 256 == 0 else hidden
    steps = hidden // chunk
    whole_block = pl.BlockSpec((CAP, width), lambda i: (0, 0))
    whole_feat = pl.BlockSpec((rows, chip_width), lambda i: (0, 0))
    col = pl.BlockSpec((rows, chunk), lambda i: (0, i))

    def weight_col(j):
        return pl.BlockSpec((1, width, chunk), lambda i, j=j: (j, 0, i))

    forward = pl.pallas_call(
        functools.partial(forward_kernel, experts, zs),
        grid=(steps,),
        out_shape=[shape_of((rows, hidden), F32)] * 2
        + [shape_of((rows, hidden))]
        + [shape_of((rows, chip_width))] * zs,
        in_specs=[SMEM] + [whole_block] * experts + [weight_col(0), weight_col(1)],
        out_specs=[col] * 3 + [whole_feat] * zs,
        scratch_shapes=[pltpu.VMEM((rows, width), BF16)],
        cost_estimate=cost(4 * rows * width * hidden, 4 * width * hidden),
        name="forward",
    )(where, *x_blocks, weights, weights)
    gate, up, hid = forward[:3]
    x_feats = forward[3:]

    backward = pl.pallas_call(
        functools.partial(backward_kernel, experts, zs),
        grid=(steps,),
        out_shape=[shape_of((rows, hidden))] * 2 + [shape_of((rows, chip_width))] * zs,
        in_specs=[SMEM] + [whole_block] * experts + [weight_col(2), col, col],
        out_specs=[col] * 2 + [whole_feat] * zs,
        scratch_shapes=[pltpu.VMEM((rows, width), BF16)],
        cost_estimate=cost(2 * rows * width * hidden, 2 * width * hidden),
        name="backward",
    )(where, *dy_blocks, weights, gate, up)
    gg, ug = backward[:2]
    dy_feats = backward[2:]

    hid_all = spread_z(hid)
    dy_all = [dy_feats[0]] + [swap_z(dy_feats[m], m) for m in range(1, zs)]
    x_all = [x_feats[0]] + [swap_z(x_feats[m], m) for m in range(1, zs)]
    gg_all = spread_z(gg)
    ug_all = spread_z(ug)

    dchunk = 512 if width % 512 == 0 else width

    def weight_row(j):
        return pl.BlockSpec((1, dchunk, hidden), lambda i, j=j: (j, i, 0))

    full = pl.BlockSpec((rows, hidden), lambda i: (0, 0))
    results = pl.pallas_call(
        functools.partial(output_kernel, experts),
        grid=(width // dchunk,),
        out_shape=[shape_of((2, CAP, width))] * experts,
        in_specs=[full] * 3 + [weight_row(0), weight_row(1), weight_row(2)],
        out_specs=[pl.BlockSpec((2, CAP, dchunk), lambda i: (0, 0, i))] * experts,
        cost_estimate=cost(6 * rows * width * hidden, 6 * width * hidden),
        name="output",
    )(hid, gg, ug, weights, weights, weights)
    back = {m: swap_expert(results[m], m) for m in [0] + order}
    mixed, grad_tokens, gates = pl.pallas_call(
        functools.partial(combine_kernel, experts),
        out_shape=[
            shape_of((tok_rows, width)),
            shape_of((tok_rows, width)),
            shape_of(ids.shape, F32),
        ],
        in_specs=[SMEM] + [VMEM] * (3 + experts),
        out_specs=[VMEM] * 3,
        cost_estimate=cost(8 * rows * tok_rows * width, 16 * tok_rows * width),
        name="combine",
    )(where, ids, probs, cotangent, *[back[m] for m in range(experts)])

    def weight_grad(feats, pieces, name):
        picks = tuple(len(p) for p in pieces)
        flat = [a for p in pieces for a in p]
        return pl.pallas_call(
            functools.partial(weight_kernel, zs, picks),
            out_shape=[
                shape_of((chip_width // CORES, hidden), F32),
                shape_of((chip_width // CORES, hidden)),
            ],
            in_specs=[VMEM] * (zs + len(flat)),
            out_specs=[VMEM] * 2,
            cost_estimate=cost(
                2 * zs * rows * chip_width * hidden, 2 * zs * rows * (hidden + chip_width)
            ),
            name=name,
        )(*feats, *flat)

    down_own, down_send = weight_grad(dy_all, hid_all, "down_grad")
    gate_own, gate_send = weight_grad(x_all, gg_all, "gate_grad")
    up_own, up_send = weight_grad(x_all, ug_all, "up_grad")
    partner = [(i, i ^ 1) for i in range(groups)]
    got = [lax.ppermute(a, "dp", partner) for a in (gate_send, up_send, down_send)]
    grads = pl.pallas_call(
        final_kernel,
        out_shape=shape_of((3, width // groups, hidden)),
        in_specs=[VMEM] * 6,
        out_specs=VMEM,
        cost_estimate=cost(3 * width * hidden // groups, 24 * width * hidden // groups),
        name="final",
    )(gate_own, up_own, down_own, *got)
    grad_weights = jnp.transpose(grads, (1, 0, 2))[:, None]
    return mixed, grad_tokens, gates.T, grad_weights


def solution(mesh):
    both = P(("dp", "expert"), None)
    return jax.shard_map(
        per_device,
        mesh=mesh,
        in_specs=(both, both, both, both, P(None, "expert", None, None)),
        out_specs=(both, both, both, P("dp", "expert", None, None)),
        check_vma=False,
    )
```

```python
import functools

import jax
import jax.numpy as jnp
from jax import lax
from jax.experimental import pallas as pl
from jax.experimental.pallas import tpu as pltpu
from jax.sharding import PartitionSpec as P

CAP = 24
CORES = 2
F32 = jnp.float32
BF16 = jnp.bfloat16
VMEM = pl.BlockSpec(memory_space=pltpu.VMEM)
HBM = pl.BlockSpec(memory_space=pltpu.HBM)
NT = (((1,), (1,)), ((), ()))
TN = (((0,), (0,)), ((), ()))


def shape_of(dims, dtype=BF16):
    return jax.ShapeDtypeStruct(dims, dtype)


def local_call(body, outs, args, flops, scratch=(), megabytes=24, space=VMEM):
    moved = sum(a.size * a.dtype.itemsize for a in list(args) + list(outs))
    return pl.pallas_call(
        body,
        out_shape=outs,
        in_specs=[space] * len(args),
        out_specs=[VMEM] * len(outs),
        scratch_shapes=list(scratch),
        compiler_params=pltpu.CompilerParams(vmem_limit_bytes=megabytes << 20),
        cost_estimate=pl.CostEstimate(
            flops=int(flops), bytes_accessed=int(moved), transcendentals=0
        ),
    )(*args)


def slot_map(ids, probs, me, experts):
    tokens = ids.shape[1]
    before = (
        lax.broadcasted_iota(jnp.int32, (tokens, tokens), 0)
        < lax.broadcasted_iota(jnp.int32, (tokens, tokens), 1)
    ).astype(BF16)
    named = []
    weight = []
    for m in range(experts):
        hit = ids == jnp.bitwise_xor(me, m)
        named.append(jnp.sum(hit.astype(F32), axis=0, keepdims=True))
        weight.append(jnp.sum(jnp.where(hit, probs, 0.0), axis=0, keepdims=True))
    mask = jnp.concatenate(named, axis=0)
    pos = jnp.dot(mask.astype(BF16), before, preferred_element_type=F32)
    rank = lax.broadcasted_iota(jnp.int32, (CAP, tokens), 0).astype(F32)
    blocks = []
    slot_probs = []
    for m in range(experts):
        hot = jnp.where((rank == pos[m : m + 1]) & (mask[m : m + 1] > 0.5), 1.0, 0.0)
        blocks.append(hot)
        slot_probs.append(jnp.sum(hot * weight[m], axis=1, keepdims=True))
    return jnp.concatenate(blocks, axis=0), jnp.concatenate(slot_probs, axis=0)


def stage_kernel(w_ref, out_ref, sem):
    copies = [
        pltpu.make_async_copy(w_ref.at[j], out_ref.at[j], sem.at[j])
        for j in range(w_ref.shape[0])
    ]
    for copy in copies:
        copy.start()
    for copy in copies:
        copy.wait()


def send_kernel(experts, zs, *refs):
    sources, refs = refs[:4], refs[4:]
    rows_out, feats_out = refs[:experts], refs[experts : experts + zs]
    scratch = refs[experts + zs : experts + zs + 2]
    held, sem = refs[experts + zs + 2 : -1], refs[-1]
    copies = [
        pltpu.make_async_copy(a, b, sem.at[j]) for j, (a, b) in enumerate(zip(sources, held))
    ]
    for copy in copies:
        copy.start()
    for copy in copies:
        copy.wait()
    ids_ref, probs_ref, tok_ref, cot_ref = held
    me = lax.axis_index("expert")
    dp = lax.axis_index("dp")
    z, c = dp // CORES, dp % CORES
    onehot, slot_probs = slot_map(ids_ref[...], probs_ref[...], me, experts)
    pick = onehot.astype(BF16)
    x_rows = jnp.dot(pick, tok_ref[...], preferred_element_type=F32)
    dy_rows = slot_probs * jnp.dot(pick, cot_ref[...], preferred_element_type=F32)
    part = x_rows.shape[1] // (zs * CORES)
    for j, value in enumerate((x_rows, dy_rows)):
        for m in range(experts):
            rows_out[m][j] = value[m * CAP : (m + 1) * CAP].astype(BF16)
        scratch[j][...] = value
        for m in range(zs):
            chip = jnp.bitwise_xor(z, m) * CORES
            for h in range(CORES):
                start = (chip + jnp.bitwise_xor(c, h)) * part
                piece = scratch[j][:, pl.ds(pl.multiple_of(start, part), part)]
                at = (j * CORES + h) * part
                for k in range(experts):
                    feats_out[m][k, :, at : at + part] = piece[
                        k * CAP : (k + 1) * CAP
                    ].astype(BF16)


def stack_rows(blocks):
    return jnp.concatenate([b.astype(F32) for b in blocks], axis=0).astype(BF16)


def ffn_kernel(experts, w_ref, *refs):
    blocks, out_ref = refs[:experts], refs[experts]
    hidden = w_ref.shape[2]
    x = stack_rows([b[0] for b in blocks])
    dy = stack_rows([b[1] for b in blocks])
    gate = jnp.dot(x, w_ref[0], preferred_element_type=F32)
    up = jnp.dot(x, w_ref[1], preferred_element_type=F32)
    s = jax.nn.sigmoid(gate)
    out_ref[:, 0:hidden] = (gate * s * up).astype(BF16)
    grad = jnp.dot(dy, w_ref[2], preferred_element_type=F32)
    out_ref[:, hidden : 2 * hidden] = (grad * up * s * (1.0 + gate * (1.0 - s))).astype(BF16)
    out_ref[:, 2 * hidden :] = (grad * (gate * s)).astype(BF16)


def output_kernel(experts, w_ref, acts_ref, *outs):
    hidden = w_ref.shape[2]
    hid, gg = acts_ref[:, 0:hidden], acts_ref[:, hidden : 2 * hidden]
    ug = acts_ref[:, 2 * hidden :]
    out = lax.dot_general(hid, w_ref[2], NT, preferred_element_type=F32)
    part = lax.dot_general(gg, w_ref[0], NT, preferred_element_type=F32)
    part += lax.dot_general(ug, w_ref[1], NT, preferred_element_type=F32)
    for m in range(experts):
        outs[m][0] = out[m * CAP : (m + 1) * CAP].astype(BF16)
        outs[m][1] = part[m * CAP : (m + 1) * CAP].astype(BF16)


def combine_kernel(experts, ids_ref, probs_ref, cot_ref, *refs):
    blocks, (mixed_ref, gtok_ref, gates_ref) = refs[:experts], refs[experts:]
    ids = ids_ref[...]
    me = lax.axis_index("expert")
    onehot, slot_probs = slot_map(ids, probs_ref[...], me, experts)
    pick = onehot.astype(BF16)
    out = jnp.concatenate([b[0].astype(F32) for b in blocks], axis=0)
    weighted = out * slot_probs
    high = weighted.astype(BF16)
    low = (weighted - high.astype(F32)).astype(BF16)
    mixed = lax.dot_general(pick, high, TN, preferred_element_type=F32)
    mixed += lax.dot_general(pick, low, TN, preferred_element_type=F32)
    mixed_ref[...] = mixed.astype(BF16)
    part = stack_rows([b[1] for b in blocks])
    gtok = lax.dot_general(pick, part, TN, preferred_element_type=F32)
    gtok_ref[...] = gtok.astype(BF16)
    cot_rows = jnp.dot(pick, cot_ref[...], preferred_element_type=F32)
    inner = jnp.sum(out * cot_rows, axis=1, keepdims=True)
    spread = onehot * inner
    gates = jnp.zeros(ids.shape, F32)
    for m in range(experts):
        value = jnp.sum(spread[m * CAP : (m + 1) * CAP], axis=0, keepdims=True)
        gates = jnp.where(ids == jnp.bitwise_xor(me, m), value, gates)
    gates_ref[...] = gates


def regroup_kernel(experts, zs, *refs):
    for k in range(experts):
        for m in range(zs):
            refs[zs + k][m] = refs[m][k]


def grad_sums(feats, acts, at):
    rows_f = stack_rows([f[m] for m in at for f in feats])
    rows_a = acts[0]
    for more in acts[1:]:
        rows_a = jnp.concatenate([rows_a, more], axis=0)
    half = rows_f.shape[1] // 2
    hidden = rows_a.shape[1] // 3
    both = lax.dot_general(
        rows_f[:, :half], rows_a[:, hidden:], TN, preferred_element_type=F32
    )
    down = lax.dot_general(
        rows_f[:, half:], rows_a[:, :hidden], TN, preferred_element_type=F32
    )
    return both, down


def early_grad_kernel(experts, at, *refs):
    feats, acts, total = refs[:experts], refs[experts:-1], refs[-1]
    both, down = grad_sums(feats, [a[...] for a in acts], at)
    total[:, : both.shape[1]] = both
    total[:, both.shape[1] :] = down


def late_grad_kernel(experts, at, *refs):
    feats, (total, *acts), (own, send) = refs[:experts], refs[experts:-2], refs[-2:]
    last = acts[0][...].astype(F32)
    for more in acts[1:]:
        last += more[...].astype(F32)
    both, down = grad_sums(feats, [last.astype(BF16)], at)
    half = both.shape[0] // CORES
    n = both.shape[1]
    own[:, :n] = total[:half, :n] + both[:half]
    own[:, n:] = total[:half, n:] + down[:half]
    send[:, :n] = (total[half:, :n] + both[half:]).astype(BF16)
    send[:, n:] = (total[half:, n:] + down[half:]).astype(BF16)


def final_kernel(own, got, out):
    hidden = out.shape[2]
    for j in range(3):
        at = slice(j * hidden, (j + 1) * hidden)
        out[j] = (own[:, at] + got[:, at].astype(F32)).astype(BF16)


def per_device(tokens, expert_ids, gate_probs, cotangent, expert_weights):
    tok_rows, width = tokens.shape
    experts = lax.axis_size("expert")
    groups = lax.axis_size("dp")
    zs = groups // CORES
    hidden = expert_weights.shape[3]
    rows = experts * CAP
    chip_width = width // zs
    weights = jnp.transpose(expert_weights[:, 0], (1, 0, 2))
    ids, probs = expert_ids.T, gate_probs.T

    def swap_expert(blocks):
        moved = list(blocks)
        for m in range(experts - 1, 0, -1):
            pairs = [(i, i ^ m) for i in range(experts)]
            moved[m] = lax.ppermute(blocks[m], "expert", pairs)
        return moved

    def swap_z(block, m, only=None):
        pairs = []
        for z in range(zs):
            if only is None or z in only:
                pairs += [(z * CORES + c, (z ^ m) * CORES + c) for c in range(CORES)]
        return lax.ppermute(block, "dp", pairs)

    def spread_z(block):
        if zs != 4:
            return [[swap_z(block, m)] for m in range(1, zs)]
        far = swap_z(block, 2)
        near = swap_z(block, 1)
        middle = swap_z(block, 3, (1, 2))
        ends = swap_z(far, 1, (1, 2))
        return [[near], [far], [middle, ends]]

    sent = local_call(
        functools.partial(send_kernel, experts, zs),
        [shape_of((2, CAP, width))] * experts + [shape_of((experts, CAP, 2 * chip_width))] * zs,
        [ids, probs, tokens, cotangent],
        4 * rows * tok_rows * width,
        [pltpu.VMEM((rows, width), F32)] * 2
        + [pltpu.VMEM(a.shape, a.dtype) for a in (ids, probs, tokens, cotangent)]
        + [pltpu.SemaphoreType.DMA((4,))],
        space=HBM,
    )
    (staged,) = local_call(
        stage_kernel,
        [shape_of(weights.shape)],
        [weights],
        0,
        [pltpu.SemaphoreType.DMA((3,))],
        space=HBM,
    )
    blocks = swap_expert(sent[:experts])
    shares = [sent[experts]] + [swap_z(sent[experts + m], m) for m in range(1, zs)]

    (acts,) = local_call(
        functools.partial(ffn_kernel, experts),
        [shape_of((rows, 3 * hidden))],
        [staged, *blocks],
        6 * rows * width * hidden,
    )
    near_far = spread_z(acts)
    results = local_call(
        functools.partial(output_kernel, experts),
        [shape_of((2, CAP, width))] * experts,
        [staged, acts],
        6 * rows * width * hidden,
    )
    back = swap_expert(results)
    by_expert = local_call(
        functools.partial(regroup_kernel, experts, zs),
        [shape_of((zs, CAP, 2 * chip_width))] * experts,
        shares,
        0,
    )
    feats = swap_expert(by_expert)
    mixed, grad_tokens, gates = local_call(
        functools.partial(combine_kernel, experts),
        [shape_of((tok_rows, width)), shape_of((tok_rows, width)), shape_of(ids.shape, F32)],
        [ids, probs, cotangent, *back],
        8 * rows * tok_rows * width,
    )
    early = near_far[:-1]
    (total,) = local_call(
        functools.partial(early_grad_kernel, experts, tuple(range(zs - 1))),
        [shape_of((chip_width, 3 * hidden), F32)],
        [*feats, acts, *[a for piece in early for a in piece]],
        6 * (zs - 1) * rows * chip_width * hidden,
    )
    own, send = local_call(
        functools.partial(late_grad_kernel, experts, (zs - 1,)),
        [
            shape_of((chip_width // CORES, 3 * hidden), F32),
            shape_of((chip_width // CORES, 3 * hidden)),
        ],
        [*feats, total, *near_far[-1]],
        6 * rows * chip_width * hidden,
    )
    got = lax.ppermute(send, "dp", [(i, i ^ 1) for i in range(groups)])
    (grads,) = local_call(
        final_kernel,
        [shape_of((3, width // groups, hidden))],
        [own, got],
        3 * width * hidden // groups,
    )
    grad_weights = jnp.transpose(grads, (1, 0, 2))[:, None]
    return mixed, grad_tokens, gates.T, grad_weights


def solution(mesh):
    both = P(("dp", "expert"), None)
    return jax.shard_map(
        per_device,
        mesh=mesh,
        in_specs=(both, both, both, both, P(None, "expert", None, None)),
        out_specs=(both, both, both, P("dp", "expert", None, None)),
        check_vma=False,
    )
```

```python
import functools

import jax
import jax.numpy as jnp
from jax import lax
from jax.experimental import pallas as pl
from jax.experimental.pallas import tpu as pltpu
from jax.sharding import PartitionSpec as P

CAP = 24
CORES = 2
PIECES = 2
SEND_MB = 24
F32 = jnp.float32
BF16 = jnp.bfloat16
VMEM = pl.BlockSpec(memory_space=pltpu.VMEM)
HBM = pl.BlockSpec(memory_space=pltpu.HBM)
NT = (((1,), (1,)), ((), ()))
TN = (((0,), (0,)), ((), ()))


def shape_of(dims, dtype=BF16):
    return jax.ShapeDtypeStruct(dims, dtype)


def local_call(body, outs, args, flops, scratch=(), megabytes=24, space=VMEM):
    moved = sum(a.size * a.dtype.itemsize for a in list(args) + list(outs))
    call = pl.pallas_call(
        body,
        out_shape=outs,
        in_specs=[space] * len(args),
        out_specs=[VMEM] * len(outs),
        scratch_shapes=list(scratch),
        compiler_params=pltpu.CompilerParams(vmem_limit_bytes=megabytes << 20),
        cost_estimate=pl.CostEstimate(
            flops=int(flops), bytes_accessed=int(moved), transcendentals=0
        ),
    )
    if space is HBM:
        args = [pltpu.with_memory_space_constraint(a, pltpu.HBM) for a in args]
    return call(*args)


def slot_map(ids, probs, me, experts):
    tokens = ids.shape[1]
    before = (
        lax.broadcasted_iota(jnp.int32, (tokens, tokens), 0)
        < lax.broadcasted_iota(jnp.int32, (tokens, tokens), 1)
    ).astype(BF16)
    named = []
    weight = []
    for m in range(experts):
        hit = ids == jnp.bitwise_xor(me, m)
        named.append(jnp.sum(hit.astype(F32), axis=0, keepdims=True))
        weight.append(jnp.sum(jnp.where(hit, probs, 0.0), axis=0, keepdims=True))
    mask = jnp.concatenate(named, axis=0)
    pos = jnp.dot(mask.astype(BF16), before, preferred_element_type=F32)
    rank = lax.broadcasted_iota(jnp.int32, (CAP, tokens), 0).astype(F32)
    blocks = []
    slot_probs = []
    for m in range(experts):
        hot = jnp.where((rank == pos[m : m + 1]) & (mask[m : m + 1] > 0.5), 1.0, 0.0)
        blocks.append(hot)
        slot_probs.append(jnp.sum(hot * weight[m], axis=1, keepdims=True))
    return jnp.concatenate(blocks, axis=0), jnp.concatenate(slot_probs, axis=0)


def stage_kernel(w_ref, out_ref, sem):
    copies = [
        pltpu.make_async_copy(w_ref.at[j], out_ref.at[j], sem.at[j])
        for j in range(w_ref.shape[0])
    ]
    for copy in copies:
        copy.start()
    for copy in copies:
        copy.wait()


def send_kernel(experts, zs, *refs):
    sources, refs = refs[:4], refs[4:]
    rows_out, feats_out = refs[:experts], refs[experts : experts + zs]
    scratch = refs[experts + zs : experts + zs + 2]
    held, sem = refs[experts + zs + 2 : -1], refs[-1]
    copies = [
        pltpu.make_async_copy(a, b, sem.at[j]) for j, (a, b) in enumerate(zip(sources, held))
    ]
    for copy in copies:
        copy.start()
    for copy in copies:
        copy.wait()
    ids_ref, probs_ref, tok_ref, cot_ref = held
    me = lax.axis_index("expert")
    dp = lax.axis_index("dp")
    z, c = dp // CORES, dp % CORES
    onehot, slot_probs = slot_map(ids_ref[...], probs_ref[...], me, experts)
    pick = onehot.astype(BF16)
    x_rows = jnp.dot(pick, tok_ref[...], preferred_element_type=F32)
    dy_rows = slot_probs * jnp.dot(pick, cot_ref[...], preferred_element_type=F32)
    part = x_rows.shape[1] // (zs * CORES)
    for j, value in enumerate((x_rows, dy_rows)):
        for m in range(experts):
            rows_out[m][j] = value[m * CAP : (m + 1) * CAP].astype(BF16)
        scratch[j][...] = value
        for m in range(zs):
            chip = jnp.bitwise_xor(z, m) * CORES
            for h in range(CORES):
                start = (chip + jnp.bitwise_xor(c, h)) * part
                piece = scratch[j][:, pl.ds(pl.multiple_of(start, part), part)]
                at = (j * CORES + h) * part
                for k in range(experts):
                    feats_out[m][k, :, at : at + part] = piece[
                        k * CAP : (k + 1) * CAP
                    ].astype(BF16)


def stack_rows(blocks):
    return jnp.concatenate([b.astype(F32) for b in blocks], axis=0).astype(BF16)


def put_columns(outs, cuts, lo, value):
    hi = lo + value.shape[1]
    for out, (at, end) in zip(outs, cuts):
        a, b = max(at, lo), min(end, hi)
        if a < b:
            out[:, a - at : b - at] = value[:, a - lo : b - lo]


def get_columns(refs, cuts, lo, hi):
    parts = []
    for ref, (at, end) in zip(refs, cuts):
        a, b = max(at, lo), min(end, hi)
        if a < b:
            parts.append(ref[:, a - at : b - at])
    return parts[0] if len(parts) == 1 else jnp.concatenate(parts, axis=1)


def ffn_kernel(experts, cuts, w_ref, *refs):
    blocks, outs = refs[:experts], refs[experts:]
    hidden = w_ref.shape[2]
    x = stack_rows([b[0] for b in blocks])
    dy = stack_rows([b[1] for b in blocks])
    gate = jnp.dot(x, w_ref[0], preferred_element_type=F32)
    up = jnp.dot(x, w_ref[1], preferred_element_type=F32)
    s = jax.nn.sigmoid(gate)
    put_columns(outs, cuts, 0, (gate * s * up).astype(BF16))
    grad = jnp.dot(dy, w_ref[2], preferred_element_type=F32)
    gate_grad = grad * up * s * (1.0 + gate * (1.0 - s))
    put_columns(outs, cuts, hidden, gate_grad.astype(BF16))
    put_columns(outs, cuts, 2 * hidden, (grad * (gate * s)).astype(BF16))


def output_kernel(experts, cuts, w_ref, *refs):
    acts, outs = refs[: len(cuts)], refs[len(cuts) :]
    hidden = w_ref.shape[2]
    hid, gg, ug = (get_columns(acts, cuts, j * hidden, (j + 1) * hidden) for j in range(3))
    out = lax.dot_general(hid, w_ref[2], NT, preferred_element_type=F32)
    part = lax.dot_general(gg, w_ref[0], NT, preferred_element_type=F32)
    part += lax.dot_general(ug, w_ref[1], NT, preferred_element_type=F32)
    for m in range(experts):
        outs[m][0] = out[m * CAP : (m + 1) * CAP].astype(BF16)
        outs[m][1] = part[m * CAP : (m + 1) * CAP].astype(BF16)


def combine_kernel(experts, ids_ref, probs_ref, cot_ref, *refs):
    blocks, (mixed_ref, gtok_ref, gates_ref) = refs[:experts], refs[experts:]
    ids = ids_ref[...]
    me = lax.axis_index("expert")
    onehot, slot_probs = slot_map(ids, probs_ref[...], me, experts)
    pick = onehot.astype(BF16)
    out = jnp.concatenate([b[0].astype(F32) for b in blocks], axis=0)
    weighted = out * slot_probs
    high = weighted.astype(BF16)
    low = (weighted - high.astype(F32)).astype(BF16)
    mixed = lax.dot_general(pick, high, TN, preferred_element_type=F32)
    mixed += lax.dot_general(pick, low, TN, preferred_element_type=F32)
    mixed_ref[...] = mixed.astype(BF16)
    part = stack_rows([b[1] for b in blocks])
    gtok = lax.dot_general(pick, part, TN, preferred_element_type=F32)
    gtok_ref[...] = gtok.astype(BF16)
    cot_rows = jnp.dot(pick, cot_ref[...], preferred_element_type=F32)
    inner = jnp.sum(out * cot_rows, axis=1, keepdims=True)
    spread = onehot * inner
    gates = jnp.zeros(ids.shape, F32)
    for m in range(experts):
        value = jnp.sum(spread[m * CAP : (m + 1) * CAP], axis=0, keepdims=True)
        gates = jnp.where(ids == jnp.bitwise_xor(me, m), value, gates)
    gates_ref[...] = gates


def regroup_kernel(experts, zs, *refs):
    for k in range(experts):
        for m in range(zs):
            refs[zs + k][m] = refs[m][k]


def grad_sums(feats, chips, picks, refs, cut):
    lo, hi, hidden = cut
    rows_f = stack_rows([f[m] for m in chips for f in feats])
    acts = []
    for n in picks:
        value = refs[0][...]
        for more in refs[1:n]:
            value += more[...]
        acts.append(value)
        refs = refs[n:]
    rows_a = acts[0] if len(acts) == 1 else jnp.concatenate(acts, axis=0)
    half = rows_f.shape[1] // 2
    sums = []
    split = min(max(hidden - lo, 0), hi - lo)
    if split > 0:
        sums.append(
            lax.dot_general(rows_f[:, half:], rows_a[:, :split], TN, preferred_element_type=F32)
        )
    if split < hi - lo:
        sums.append(
            lax.dot_general(rows_f[:, :half], rows_a[:, split:], TN, preferred_element_type=F32)
        )
    return sums[0] if len(sums) == 1 else jnp.concatenate(sums, axis=1)


def early_grad_kernel(experts, chips, picks, cut, *refs):
    feats, acts, total = refs[:experts], refs[experts:-1], refs[-1]
    total[...] = grad_sums(feats, chips, picks, acts, cut)


def late_grad_kernel(experts, chips, picks, cut, *refs):
    feats, (total, *acts), (own, send) = refs[:experts], refs[experts:-2], refs[-2:]
    more = grad_sums(feats, chips, picks, acts, cut)
    half = more.shape[0] // CORES
    own[...] = total[:half] + more[:half]
    send[...] = (total[half:] + more[half:]).astype(BF16)


def final_kernel(cuts, *refs):
    n = len(cuts)
    owns, gots, out = refs[:n], refs[n : 2 * n], refs[-1]
    hidden = out.shape[2]
    for k, (lo, hi) in enumerate(cuts):
        value = (owns[k][...] + gots[k][...].astype(F32)).astype(BF16)
        for j in range(3):
            a, b = max(lo, j * hidden), min(hi, (j + 1) * hidden)
            if a < b:
                out[(j + 2) % 3, :, a - j * hidden : b - j * hidden] = value[:, a - lo : b - lo]


def per_device(tokens, expert_ids, gate_probs, cotangent, expert_weights):
    tok_rows, width = tokens.shape
    experts = lax.axis_size("expert")
    groups = lax.axis_size("dp")
    zs = groups // CORES
    hidden = expert_weights.shape[3]
    rows = experts * CAP
    chip_width = width // zs
    weights = jnp.transpose(expert_weights[:, 0], (1, 0, 2))
    ids, probs = expert_ids.T, gate_probs.T

    def swap_expert(blocks):
        moved = list(blocks)
        for m in range(experts - 1, 0, -1):
            pairs = [(i, i ^ m) for i in range(experts)]
            moved[m] = lax.ppermute(blocks[m], "expert", pairs)
        return moved

    def swap_z(block, m, only=None):
        pairs = []
        for z in range(zs):
            if only is None or z in only:
                pairs += [(z * CORES + c, (z ^ m) * CORES + c) for c in range(CORES)]
        return lax.ppermute(block, "dp", pairs)

    def spread_z(block):
        if zs != 4:
            return [[swap_z(block, m)] for m in range(1, zs)]
        near = swap_z(block, 1)
        middle = swap_z(block, 3, (1, 2))
        through = swap_z(near, 3, (1, 2))
        ends = swap_z(middle, 1, (1, 2))
        last = swap_z(through, 1, (1, 2))
        return [[near], [through, ends], [middle, last]]

    sent = local_call(
        functools.partial(send_kernel, experts, zs),
        [shape_of((2, CAP, width))] * experts + [shape_of((experts, CAP, 2 * chip_width))] * zs,
        [ids, probs, tokens, cotangent],
        4 * rows * tok_rows * width,
        [pltpu.VMEM((rows, width), F32)] * 2
        + [pltpu.VMEM(a.shape, a.dtype) for a in (ids, probs, tokens, cotangent)]
        + [pltpu.SemaphoreType.DMA((4,))],
        space=HBM,
        megabytes=SEND_MB,
    )
    (staged,) = local_call(
        stage_kernel,
        [shape_of(weights.shape)],
        [weights],
        0,
        [pltpu.SemaphoreType.DMA((3,))],
        space=HBM,
    )
    blocks = swap_expert(sent[:experts])
    shares = [sent[experts]] + [swap_z(sent[experts + m], m) for m in range(1, zs)]

    step = 3 * hidden // PIECES
    cuts = [(k * step, (k + 1) * step) for k in range(PIECES)]
    acts = local_call(
        functools.partial(ffn_kernel, experts, cuts),
        [shape_of((rows, step))] * PIECES,
        [staged, *blocks],
        6 * rows * width * hidden,
    )
    spread = [spread_z(block) for block in acts]
    results = local_call(
        functools.partial(output_kernel, experts, cuts),
        [shape_of((2, CAP, width))] * experts,
        [staged, *acts],
        6 * rows * width * hidden,
    )
    back = swap_expert(results)
    by_expert = local_call(
        functools.partial(regroup_kernel, experts, zs),
        [shape_of((zs, CAP, 2 * chip_width))] * experts,
        shares,
        0,
    )
    feats = swap_expert(by_expert)
    mixed, grad_tokens, gates = local_call(
        functools.partial(combine_kernel, experts),
        [shape_of((tok_rows, width)), shape_of((tok_rows, width)), shape_of(ids.shape, F32)],
        [ids, probs, cotangent, *back],
        8 * rows * tok_rows * width,
    )
    owns, gots = [], []
    for k in range(PIECES):
        cut = (*cuts[k], hidden)
        pieces = [[acts[k]]] + spread[k][:-1]
        (total,) = local_call(
            functools.partial(
                early_grad_kernel, experts, tuple(range(zs - 1)), tuple(map(len, pieces)), cut
            ),
            [shape_of((chip_width, step), F32)],
            [*feats, *[a for piece in pieces for a in piece]],
            2 * (zs - 1) * rows * chip_width * step,
        )
        pieces = spread[k][-1]
        own, send = local_call(
            functools.partial(late_grad_kernel, experts, (zs - 1,), (len(pieces),), cut),
            [
                shape_of((chip_width // CORES, step), F32),
                shape_of((chip_width // CORES, step)),
            ],
            [*feats, total, *pieces],
            2 * rows * chip_width * step,
        )
        gots.append(lax.ppermute(send, "dp", [(i, i ^ 1) for i in range(groups)]))
        owns.append(own)
    (grads,) = local_call(
        functools.partial(final_kernel, cuts),
        [shape_of((3, width // groups, hidden))],
        [*owns, *gots],
        3 * width * hidden // groups,
    )
    grad_weights = jnp.transpose(grads, (1, 0, 2))[:, None]
    return mixed, grad_tokens, gates.T, grad_weights


def solution(mesh):
    both = P(("dp", "expert"), None)
    return jax.shard_map(
        per_device,
        mesh=mesh,
        in_specs=(both, both, both, both, P(None, "expert", None, None)),
        out_specs=(both, both, both, P("dp", "expert", None, None)),
        check_vma=False,
    )
```

```python
import functools

import jax
import jax.numpy as jnp
from jax import lax
from jax.experimental import pallas as pl
from jax.experimental.pallas import tpu as pltpu
from jax.sharding import PartitionSpec as P

CAP = 24
CORES = 2
PIECES = 2
SEND_MB = 24
F32 = jnp.float32
BF16 = jnp.bfloat16
VMEM = pl.BlockSpec(memory_space=pltpu.VMEM)
HBM = pl.BlockSpec(memory_space=pltpu.HBM)
NT = (((1,), (1,)), ((), ()))
TN = (((0,), (0,)), ((), ()))


def shape_of(dims, dtype=BF16):
    return jax.ShapeDtypeStruct(dims, dtype)


def local_call(body, outs, args, flops, scratch=(), megabytes=24, space=VMEM):
    moved = sum(a.size * a.dtype.itemsize for a in list(args) + list(outs))
    call = pl.pallas_call(
        body,
        out_shape=outs,
        in_specs=[space] * len(args),
        out_specs=[VMEM] * len(outs),
        scratch_shapes=list(scratch),
        compiler_params=pltpu.CompilerParams(vmem_limit_bytes=megabytes << 20),
        cost_estimate=pl.CostEstimate(
            flops=int(flops), bytes_accessed=int(moved), transcendentals=0
        ),
    )
    if space is HBM:
        args = [pltpu.with_memory_space_constraint(a, pltpu.HBM) for a in args]
    return call(*args)


def slot_map(ids, probs, me, experts):
    tokens = ids.shape[1]
    before = (
        lax.broadcasted_iota(jnp.int32, (tokens, tokens), 0)
        < lax.broadcasted_iota(jnp.int32, (tokens, tokens), 1)
    ).astype(BF16)
    named = []
    weight = []
    for m in range(experts):
        hit = ids == jnp.bitwise_xor(me, m)
        named.append(jnp.sum(hit.astype(F32), axis=0, keepdims=True))
        weight.append(jnp.sum(jnp.where(hit, probs, 0.0), axis=0, keepdims=True))
    mask = jnp.concatenate(named, axis=0)
    pos = jnp.dot(mask.astype(BF16), before, preferred_element_type=F32)
    rank = lax.broadcasted_iota(jnp.int32, (CAP, tokens), 0).astype(F32)
    blocks = []
    slot_probs = []
    for m in range(experts):
        hot = jnp.where((rank == pos[m : m + 1]) & (mask[m : m + 1] > 0.5), 1.0, 0.0)
        blocks.append(hot)
        slot_probs.append(jnp.sum(hot * weight[m], axis=1, keepdims=True))
    return jnp.concatenate(blocks, axis=0), jnp.concatenate(slot_probs, axis=0)


def stage_kernel(w_ref, out_ref, sem):
    copies = [
        pltpu.make_async_copy(w_ref.at[j], out_ref.at[j], sem.at[j])
        for j in range(w_ref.shape[0])
    ]
    for copy in copies:
        copy.start()
    for copy in copies:
        copy.wait()


def send_kernel(experts, zs, *refs):
    sources, refs = refs[:4], refs[4:]
    rows_out, feats_out = refs[:experts], refs[experts : experts + zs]
    scratch = refs[experts + zs : experts + zs + 2]
    held, sem = refs[experts + zs + 2 : -1], refs[-1]
    copies = [
        pltpu.make_async_copy(a, b, sem.at[j]) for j, (a, b) in enumerate(zip(sources, held))
    ]
    for copy in copies:
        copy.start()
    for copy in copies:
        copy.wait()
    ids_ref, probs_ref, tok_ref, cot_ref = held
    me = lax.axis_index("expert")
    dp = lax.axis_index("dp")
    z, c = dp // CORES, dp % CORES
    onehot, slot_probs = slot_map(ids_ref[...], probs_ref[...], me, experts)
    pick = onehot.astype(BF16)
    x_rows = jnp.dot(pick, tok_ref[...], preferred_element_type=F32)
    dy_rows = slot_probs * jnp.dot(pick, cot_ref[...], preferred_element_type=F32)
    part = x_rows.shape[1] // (zs * CORES)
    for j, value in enumerate((x_rows, dy_rows)):
        for m in range(experts):
            rows_out[m][j] = value[m * CAP : (m + 1) * CAP].astype(BF16)
        scratch[j][...] = value
        for m in range(zs):
            chip = jnp.bitwise_xor(z, m) * CORES
            for h in range(CORES):
                start = (chip + jnp.bitwise_xor(c, h)) * part
                piece = scratch[j][:, pl.ds(pl.multiple_of(start, part), part)]
                at = (j * CORES + h) * part
                for k in range(experts):
                    feats_out[m][k, :, at : at + part] = piece[
                        k * CAP : (k + 1) * CAP
                    ].astype(BF16)


def stack_rows(blocks):
    return jnp.concatenate([b.astype(F32) for b in blocks], axis=0).astype(BF16)


def put_columns(outs, cuts, lo, value):
    hi = lo + value.shape[1]
    for out, (at, end) in zip(outs, cuts):
        a, b = max(at, lo), min(end, hi)
        if a < b:
            out[:, a - at : b - at] = value[:, a - lo : b - lo]


def get_columns(refs, cuts, lo, hi):
    parts = []
    for ref, (at, end) in zip(refs, cuts):
        a, b = max(at, lo), min(end, hi)
        if a < b:
            parts.append(ref[:, a - at : b - at])
    return parts[0] if len(parts) == 1 else jnp.concatenate(parts, axis=1)


def ffn_kernel(experts, cuts, w_ref, *refs):
    blocks, outs = refs[:experts], refs[experts:]
    hidden = w_ref.shape[2]
    x = stack_rows([b[0] for b in blocks])
    dy = stack_rows([b[1] for b in blocks])
    gate = jnp.dot(x, w_ref[0], preferred_element_type=F32)
    up = jnp.dot(x, w_ref[1], preferred_element_type=F32)
    s = jax.nn.sigmoid(gate)
    put_columns(outs, cuts, 0, (gate * s * up).astype(BF16))
    grad = jnp.dot(dy, w_ref[2], preferred_element_type=F32)
    gate_grad = grad * up * s * (1.0 + gate * (1.0 - s))
    put_columns(outs, cuts, hidden, gate_grad.astype(BF16))
    put_columns(outs, cuts, 2 * hidden, (grad * (gate * s)).astype(BF16))


def output_kernel(experts, cuts, w_ref, *refs):
    acts, outs = refs[: len(cuts)], refs[len(cuts) :]
    hidden = w_ref.shape[2]
    hid, gg, ug = (get_columns(acts, cuts, j * hidden, (j + 1) * hidden) for j in range(3))
    out = lax.dot_general(hid, w_ref[2], NT, preferred_element_type=F32)
    part = lax.dot_general(gg, w_ref[0], NT, preferred_element_type=F32)
    part += lax.dot_general(ug, w_ref[1], NT, preferred_element_type=F32)
    for m in range(experts):
        outs[m][0] = out[m * CAP : (m + 1) * CAP].astype(BF16)
        outs[m][1] = part[m * CAP : (m + 1) * CAP].astype(BF16)


def combine_kernel(experts, ids_ref, probs_ref, cot_ref, *refs):
    blocks, (mixed_ref, gtok_ref, gates_ref) = refs[:experts], refs[experts:]
    ids = ids_ref[...]
    me = lax.axis_index("expert")
    onehot, slot_probs = slot_map(ids, probs_ref[...], me, experts)
    pick = onehot.astype(BF16)
    out = jnp.concatenate([b[0].astype(F32) for b in blocks], axis=0)
    weighted = out * slot_probs
    high = weighted.astype(BF16)
    low = (weighted - high.astype(F32)).astype(BF16)
    mixed = lax.dot_general(pick, high, TN, preferred_element_type=F32)
    mixed += lax.dot_general(pick, low, TN, preferred_element_type=F32)
    mixed_ref[...] = mixed.astype(BF16)
    part = stack_rows([b[1] for b in blocks])
    gtok = lax.dot_general(pick, part, TN, preferred_element_type=F32)
    gtok_ref[...] = gtok.astype(BF16)
    cot_rows = jnp.dot(pick, cot_ref[...], preferred_element_type=F32)
    inner = jnp.sum(out * cot_rows, axis=1, keepdims=True)
    spread = onehot * inner
    gates = jnp.zeros(ids.shape, F32)
    for m in range(experts):
        value = jnp.sum(spread[m * CAP : (m + 1) * CAP], axis=0, keepdims=True)
        gates = jnp.where(ids == jnp.bitwise_xor(me, m), value, gates)
    gates_ref[...] = gates


def regroup_kernel(experts, zs, *refs):
    results, shares, outs = refs[:experts], refs[experts : experts + zs], refs[experts + zs :]
    wide = shares[0].shape[2]
    for k in range(experts):
        outs[k][:2] = results[k][...]
        for m in range(zs):
            row, at = divmod(m * wide, results[k].shape[2])
            outs[k][2 + row, :, at : at + wide] = shares[m][k]


def features_of(message, chip, zs):
    wide = 2 * message.shape[2] // zs
    row, at = divmod(chip * wide, message.shape[2])
    return message[2 + row, :, at : at + wide]


def grad_sums(feats, chips, zs, picks, refs, cut):
    lo, hi, hidden = cut
    rows_f = stack_rows([features_of(f, m, zs) for m in chips for f in feats])
    acts = []
    for n in picks:
        value = refs[0][...]
        for more in refs[1:n]:
            value += more[...]
        acts.append(value)
        refs = refs[n:]
    rows_a = acts[0] if len(acts) == 1 else jnp.concatenate(acts, axis=0)
    half = rows_f.shape[1] // 2
    sums = []
    split = min(max(hidden - lo, 0), hi - lo)
    if split > 0:
        sums.append(
            lax.dot_general(rows_f[:, half:], rows_a[:, :split], TN, preferred_element_type=F32)
        )
    if split < hi - lo:
        sums.append(
            lax.dot_general(rows_f[:, :half], rows_a[:, split:], TN, preferred_element_type=F32)
        )
    return sums[0] if len(sums) == 1 else jnp.concatenate(sums, axis=1)


def early_grad_kernel(experts, chips, zs, picks, cut, *refs):
    feats, acts, total = refs[:experts], refs[experts:-1], refs[-1]
    total[...] = grad_sums(feats, chips, zs, picks, acts, cut)


def late_grad_kernel(experts, chips, zs, picks, cut, *refs):
    feats, (total, *acts), (own, send) = refs[:experts], refs[experts:-2], refs[-2:]
    more = grad_sums(feats, chips, zs, picks, acts, cut)
    half = more.shape[0] // CORES
    own[...] = total[:half] + more[:half]
    send[...] = (total[half:] + more[half:]).astype(BF16)


def final_kernel(cuts, *refs):
    n = len(cuts)
    owns, gots, out = refs[:n], refs[n : 2 * n], refs[-1]
    hidden = out.shape[2]
    for k, (lo, hi) in enumerate(cuts):
        value = (owns[k][...] + gots[k][...].astype(F32)).astype(BF16)
        for j in range(3):
            a, b = max(lo, j * hidden), min(hi, (j + 1) * hidden)
            if a < b:
                out[(j + 2) % 3, :, a - j * hidden : b - j * hidden] = value[:, a - lo : b - lo]


def per_device(tokens, expert_ids, gate_probs, cotangent, expert_weights):
    tok_rows, width = tokens.shape
    experts = lax.axis_size("expert")
    groups = lax.axis_size("dp")
    zs = groups // CORES
    hidden = expert_weights.shape[3]
    rows = experts * CAP
    chip_width = width // zs
    weights = jnp.transpose(expert_weights[:, 0], (1, 0, 2))
    ids, probs = expert_ids.T, gate_probs.T

    def swap_expert(blocks):
        moved = list(blocks)
        for m in range(experts - 1, 0, -1):
            pairs = [(i, i ^ m) for i in range(experts)]
            moved[m] = lax.ppermute(blocks[m], "expert", pairs)
        return moved

    def swap_z(block, m, only=None):
        pairs = []
        for z in range(zs):
            if only is None or z in only:
                pairs += [(z * CORES + c, (z ^ m) * CORES + c) for c in range(CORES)]
        return lax.ppermute(block, "dp", pairs)

    def spread_z(block):
        if zs != 4:
            return [[swap_z(block, m)] for m in range(1, zs)]
        near = swap_z(block, 1)
        middle = swap_z(block, 3, (1, 2))
        through = swap_z(near, 3, (1, 2))
        ends = swap_z(middle, 1)
        last = swap_z(through, 1)
        return [[near], [through, ends], [middle, last]]

    sent = local_call(
        functools.partial(send_kernel, experts, zs),
        [shape_of((2, CAP, width))] * experts + [shape_of((experts, CAP, 2 * chip_width))] * zs,
        [ids, probs, tokens, cotangent],
        4 * rows * tok_rows * width,
        [pltpu.VMEM((rows, width), F32)] * 2
        + [pltpu.VMEM(a.shape, a.dtype) for a in (ids, probs, tokens, cotangent)]
        + [pltpu.SemaphoreType.DMA((4,))],
        space=HBM,
        megabytes=SEND_MB,
    )
    (staged,) = local_call(
        stage_kernel,
        [shape_of(weights.shape)],
        [weights],
        0,
        [pltpu.SemaphoreType.DMA((3,))],
        space=HBM,
    )
    blocks = swap_expert(sent[:experts])
    shares = [sent[experts]] + [swap_z(sent[experts + m], m) for m in range(1, zs)]

    step = 3 * hidden // PIECES
    cuts = [(k * step, (k + 1) * step) for k in range(PIECES)]
    acts = local_call(
        functools.partial(ffn_kernel, experts, cuts),
        [shape_of((rows, step))] * PIECES,
        [staged, *blocks],
        6 * rows * width * hidden,
    )
    spread = [spread_z(block) for block in acts]
    results = local_call(
        functools.partial(output_kernel, experts, cuts),
        [shape_of((2, CAP, width))] * experts,
        [staged, *acts],
        6 * rows * width * hidden,
    )
    messages = local_call(
        functools.partial(regroup_kernel, experts, zs),
        [shape_of((4, CAP, width))] * experts,
        [*results, *shares],
        0,
    )
    back = feats = swap_expert(messages)
    mixed, grad_tokens, gates = local_call(
        functools.partial(combine_kernel, experts),
        [shape_of((tok_rows, width)), shape_of((tok_rows, width)), shape_of(ids.shape, F32)],
        [ids, probs, cotangent, *back],
        8 * rows * tok_rows * width,
    )
    owns, gots = [], []
    for k in range(PIECES):
        cut = (*cuts[k], hidden)
        pieces = [[acts[k]]] + spread[k][:-1]
        (total,) = local_call(
            functools.partial(
                early_grad_kernel,
                experts,
                tuple(range(zs - 1)),
                zs,
                tuple(map(len, pieces)),
                cut,
            ),
            [shape_of((chip_width, step), F32)],
            [*feats, *[a for piece in pieces for a in piece]],
            2 * (zs - 1) * rows * chip_width * step,
        )
        pieces = spread[k][-1]
        own, send = local_call(
            functools.partial(late_grad_kernel, experts, (zs - 1,), zs, (len(pieces),), cut),
            [
                shape_of((chip_width // CORES, step), F32),
                shape_of((chip_width // CORES, step)),
            ],
            [*feats, total, *pieces],
            2 * rows * chip_width * step,
        )
        gots.append(lax.ppermute(send, "dp", [(i, i ^ 1) for i in range(groups)]))
        owns.append(own)
    (grads,) = local_call(
        functools.partial(final_kernel, cuts),
        [shape_of((3, width // groups, hidden))],
        [*owns, *gots],
        3 * width * hidden // groups,
    )
    grad_weights = jnp.transpose(grads, (1, 0, 2))[:, None]
    return mixed, grad_tokens, gates.T, grad_weights


def solution(mesh):
    both = P(("dp", "expert"), None)
    return jax.shard_map(
        per_device,
        mesh=mesh,
        in_specs=(both, both, both, both, P(None, "expert", None, None)),
        out_specs=(both, both, both, P("dp", "expert", None, None)),
        check_vma=False,
    )
```

```python
import functools

import jax
import jax.numpy as jnp
from jax import lax
from jax.experimental import pallas as pl
from jax.experimental.pallas import tpu as pltpu
from jax.sharding import PartitionSpec as P

CAP = 24
CORES = 2
PARTS = (9, 9)
PIECES = len(PARTS)
SEND_MB = 24
F32 = jnp.float32
BF16 = jnp.bfloat16
VMEM = pl.BlockSpec(memory_space=pltpu.VMEM)
HBM = pl.BlockSpec(memory_space=pltpu.HBM)
NT = (((1,), (1,)), ((), ()))
TN = (((0,), (0,)), ((), ()))


def shape_of(dims, dtype=BF16):
    return jax.ShapeDtypeStruct(dims, dtype)


def local_call(
    body, outs, args, flops, scratch=(), megabytes=24, space=VMEM, out=VMEM, reuse=False
):
    moved = sum(a.size * a.dtype.itemsize for a in list(args) + list(outs))
    call = pl.pallas_call(
        body,
        out_shape=outs,
        in_specs=[space] * (len(args) - reuse) + [HBM] * reuse,
        out_specs=[out] * len(outs),
        input_output_aliases={len(args) - 1: 0} if reuse else {},
        scratch_shapes=list(scratch),
        compiler_params=pltpu.CompilerParams(vmem_limit_bytes=megabytes << 20),
        cost_estimate=pl.CostEstimate(
            flops=int(flops), bytes_accessed=int(moved), transcendentals=0
        ),
    )
    if space is HBM:
        args = [pltpu.with_memory_space_constraint(a, pltpu.HBM) for a in args]
    return call(*args)


def slot_map(ids, probs, me, experts):
    tokens = ids.shape[1]
    before = (
        lax.broadcasted_iota(jnp.int32, (tokens, tokens), 0)
        < lax.broadcasted_iota(jnp.int32, (tokens, tokens), 1)
    ).astype(BF16)
    named = []
    weight = []
    for m in range(experts):
        hit = ids == jnp.bitwise_xor(me, m)
        named.append(jnp.sum(hit.astype(F32), axis=0, keepdims=True))
        weight.append(jnp.sum(jnp.where(hit, probs, 0.0), axis=0, keepdims=True))
    mask = jnp.concatenate(named, axis=0)
    pos = jnp.dot(mask.astype(BF16), before, preferred_element_type=F32)
    rank = lax.broadcasted_iota(jnp.int32, (CAP, tokens), 0).astype(F32)
    blocks = []
    slot_probs = []
    for m in range(experts):
        hot = jnp.where((rank == pos[m : m + 1]) & (mask[m : m + 1] > 0.5), 1.0, 0.0)
        blocks.append(hot)
        slot_probs.append(jnp.sum(hot * weight[m], axis=1, keepdims=True))
    return jnp.concatenate(blocks, axis=0), jnp.concatenate(slot_probs, axis=0)


def stage_kernel(w_ref, out_ref, sem):
    copies = [
        pltpu.make_async_copy(w_ref.at[j], out_ref.at[j], sem.at[j])
        for j in range(w_ref.shape[0])
    ]
    for copy in copies:
        copy.start()
    for copy in copies:
        copy.wait()


def send_kernel(experts, zs, *refs):
    sources, refs = refs[:4], refs[4:]
    rows_out, feats_out = refs[:experts], refs[experts : experts + zs]
    scratch = refs[experts + zs : experts + zs + 2]
    held, sem = refs[experts + zs + 2 : -1], refs[-1]
    copies = [
        pltpu.make_async_copy(a, b, sem.at[j]) for j, (a, b) in enumerate(zip(sources, held))
    ]
    for copy in copies:
        copy.start()
    for copy in copies:
        copy.wait()
    ids_ref, probs_ref, tok_ref, cot_ref = held
    me = lax.axis_index("expert")
    dp = lax.axis_index("dp")
    z, c = dp // CORES, dp % CORES
    onehot, slot_probs = slot_map(ids_ref[...], probs_ref[...], me, experts)
    pick = onehot.astype(BF16)
    x_rows = jnp.dot(pick, tok_ref[...], preferred_element_type=F32)
    dy_rows = slot_probs * jnp.dot(pick, cot_ref[...], preferred_element_type=F32)
    part = x_rows.shape[1] // (zs * CORES)
    for j, value in enumerate((x_rows, dy_rows)):
        for m in range(experts):
            rows_out[m][j] = value[m * CAP : (m + 1) * CAP].astype(BF16)
        scratch[j][...] = value
        for m in range(zs):
            chip = jnp.bitwise_xor(z, m) * CORES
            for h in range(CORES):
                start = (chip + jnp.bitwise_xor(c, h)) * part
                piece = scratch[j][:, pl.ds(pl.multiple_of(start, part), part)]
                at = (j * CORES + h) * part
                for k in range(experts):
                    feats_out[m][k, :, at : at + part] = piece[
                        k * CAP : (k + 1) * CAP
                    ].astype(BF16)


def stack_rows(blocks):
    return jnp.concatenate([b.astype(F32) for b in blocks], axis=0).astype(BF16)


def put_columns(outs, cuts, lo, value):
    hi = lo + value.shape[1]
    for out, (at, end) in zip(outs, cuts):
        a, b = max(at, lo), min(end, hi)
        if a < b:
            out[:, a - at : b - at] = value[:, a - lo : b - lo]


def get_columns(refs, cuts, lo, hi):
    parts = []
    for ref, (at, end) in zip(refs, cuts):
        a, b = max(at, lo), min(end, hi)
        if a < b:
            parts.append(ref[:, a - at : b - at])
    return parts[0] if len(parts) == 1 else jnp.concatenate(parts, axis=1)


def ffn_kernel(experts, cuts, w_ref, *refs):
    blocks, outs = refs[:experts], refs[experts:]
    hidden = w_ref.shape[2]
    x = stack_rows([b[0] for b in blocks])
    dy = stack_rows([b[1] for b in blocks])
    gate = jnp.dot(x, w_ref[0], preferred_element_type=F32)
    up = jnp.dot(x, w_ref[1], preferred_element_type=F32)
    s = jax.nn.sigmoid(gate)
    put_columns(outs, cuts, 0, (gate * s * up).astype(BF16))
    grad = jnp.dot(dy, w_ref[2], preferred_element_type=F32)
    gate_grad = grad * up * s * (1.0 + gate * (1.0 - s))
    put_columns(outs, cuts, hidden, gate_grad.astype(BF16))
    put_columns(outs, cuts, 2 * hidden, (grad * (gate * s)).astype(BF16))


def output_kernel(experts, cuts, w_ref, *refs):
    acts, outs = refs[: len(cuts)], refs[len(cuts) :]
    hidden = w_ref.shape[2]
    hid, gg, ug = (get_columns(acts, cuts, j * hidden, (j + 1) * hidden) for j in range(3))
    out = lax.dot_general(hid, w_ref[2], NT, preferred_element_type=F32)
    part = lax.dot_general(gg, w_ref[0], NT, preferred_element_type=F32)
    part += lax.dot_general(ug, w_ref[1], NT, preferred_element_type=F32)
    for m in range(experts):
        outs[m][0] = out[m * CAP : (m + 1) * CAP].astype(BF16)
        outs[m][1] = part[m * CAP : (m + 1) * CAP].astype(BF16)


def combine_kernel(experts, ids_ref, probs_ref, cot_ref, *refs):
    blocks, (mixed_ref, gtok_ref, gates_ref) = refs[:experts], refs[experts:]
    ids = ids_ref[...]
    me = lax.axis_index("expert")
    onehot, slot_probs = slot_map(ids, probs_ref[...], me, experts)
    pick = onehot.astype(BF16)
    out = jnp.concatenate([b[0].astype(F32) for b in blocks], axis=0)
    weighted = out * slot_probs
    high = weighted.astype(BF16)
    low = (weighted - high.astype(F32)).astype(BF16)
    mixed = lax.dot_general(pick, high, TN, preferred_element_type=F32)
    mixed += lax.dot_general(pick, low, TN, preferred_element_type=F32)
    mixed_ref[...] = mixed.astype(BF16)
    part = stack_rows([b[1] for b in blocks])
    gtok = lax.dot_general(pick, part, TN, preferred_element_type=F32)
    gtok_ref[...] = gtok.astype(BF16)
    cot_rows = jnp.dot(pick, cot_ref[...], preferred_element_type=F32)
    inner = jnp.sum(out * cot_rows, axis=1, keepdims=True)
    spread = onehot * inner
    gates = jnp.zeros(ids.shape, F32)
    for m in range(experts):
        value = jnp.sum(spread[m * CAP : (m + 1) * CAP], axis=0, keepdims=True)
        gates = jnp.where(ids == jnp.bitwise_xor(me, m), value, gates)
    gates_ref[...] = gates


def regroup_kernel(experts, zs, *refs):
    results, shares, outs = refs[:experts], refs[experts : experts + zs], refs[experts + zs :]
    wide = shares[0].shape[2]
    for k in range(experts):
        outs[k][:2] = results[k][...]
        for m in range(zs):
            row, at = divmod(m * wide, results[k].shape[2])
            outs[k][2 + row, :, at : at + wide] = shares[m][k]


def features_of(message, chip, zs):
    wide = 2 * message.shape[2] // zs
    row, at = divmod(chip * wide, message.shape[2])
    return message[2 + row, :, at : at + wide]


def pick_rows(refs):
    value = refs[0][...]
    for more in refs[1:]:
        value += more[...]
    return value


def contract(rows_f, rows_a, cut):
    lo, hi, hidden = cut
    half = rows_f.shape[1] // 2
    sums = []
    split = min(max(hidden - lo, 0), hi - lo)
    if split > 0:
        sums.append(
            lax.dot_general(rows_f[:, half:], rows_a[:, :split], TN, preferred_element_type=F32)
        )
    if split < hi - lo:
        sums.append(
            lax.dot_general(rows_f[:, :half], rows_a[:, split:], TN, preferred_element_type=F32)
        )
    return sums[0] if len(sums) == 1 else jnp.concatenate(sums, axis=1)


def grad_sums(feats, chips, zs, picks, refs, cut):
    rows_f = stack_rows([features_of(f, m, zs) for m in chips for f in feats])
    acts = []
    for n in picks:
        acts.append(pick_rows(refs[:n]))
        refs = refs[n:]
    rows_a = acts[0] if len(acts) == 1 else jnp.concatenate(acts, axis=0)
    return contract(rows_f, rows_a, cut)


def early_grad_kernel(experts, chips, zs, picks, cut, *refs):
    feats, acts, total = refs[:experts], refs[experts:-1], refs[-1]
    total[...] = grad_sums(feats, chips, zs, picks, acts, cut)


def late_grad_kernel(experts, chips, zs, picks, cut, *refs):
    feats, (total, *acts), (own, send) = refs[:experts], refs[experts:-2], refs[-2:]
    more = grad_sums(feats, chips, zs, picks, acts, cut)
    half = more.shape[0] // CORES
    own[...] = total[:half] + more[:half]
    send[...] = (total[half:] + more[half:]).astype(BF16)


def last_early_kernel(experts, chips, zs, picks, cut, *refs):
    feats, acts, (own, send, feat) = refs[:experts], refs[experts:-3], refs[-3:]
    total = grad_sums(feats, chips, zs, picks, acts, cut)
    half = total.shape[0] // CORES
    own[...] = total[:half]
    send[...] = total[half:].astype(BF16)
    rows_f = stack_rows([features_of(f, zs - 1, zs) for f in feats])
    part = rows_f.shape[1] // 4
    feat[:, :part] = rows_f[:, part : 2 * part]
    feat[:, part:] = rows_f[:, 3 * part :]


def store_piece(value, cut, held, out, sem):
    lo, hi, hidden = cut
    held[...] = value.astype(BF16)
    copies = []
    for j in range(3):
        a, b = max(lo, j * hidden), min(hi, (j + 1) * hidden)
        if a < b:
            source = held.at[:, a - lo : b - lo]
            target = out.at[(j + 2) % 3, :, a - j * hidden : b - j * hidden]
            copies.append(pltpu.make_async_copy(source, target, sem.at[j]))
    for copy in copies:
        copy.start()
    for copy in copies:
        copy.wait()


def first_store_kernel(cut, own, got, *refs):
    out, held, sem = refs[-3:]
    store_piece(own[...] + got[...].astype(F32), cut, held, out, sem)


def last_store_kernel(experts, zs, picks, cut, *refs):
    feats, (own, got, other_feat) = refs[:experts], refs[experts : experts + 3]
    acts = refs[experts + 3 : experts + 3 + 2 * picks]
    _, out, held, sem = refs[experts + 3 + 2 * picks :]
    rows_f = stack_rows([features_of(f, zs - 1, zs) for f in feats])
    part = rows_f.shape[1] // 4
    mine = jnp.concatenate([rows_f[:, :part], rows_f[:, 2 * part : 3 * part]], axis=1)
    rows_f = jnp.concatenate([mine, other_feat[...]], axis=0)
    rows_a = jnp.concatenate([pick_rows(acts[:picks]), pick_rows(acts[picks:])], axis=0)
    total = own[...] + got[...].astype(F32) + contract(rows_f, rows_a, cut)
    store_piece(total, cut, held, out, sem)


def per_device(tokens, expert_ids, gate_probs, cotangent, expert_weights):
    tok_rows, width = tokens.shape
    experts = lax.axis_size("expert")
    groups = lax.axis_size("dp")
    zs = groups // CORES
    hidden = expert_weights.shape[3]
    rows = experts * CAP
    chip_width = width // zs
    weights = jnp.transpose(expert_weights[:, 0], (1, 0, 2))
    ids, probs = expert_ids.T, gate_probs.T

    def swap_expert(blocks):
        moved = list(blocks)
        for m in range(experts - 1, 0, -1):
            pairs = [(i, i ^ m) for i in range(experts)]
            moved[m] = lax.ppermute(blocks[m], "expert", pairs)
        return moved

    def swap_z(block, m, only=None):
        pairs = []
        for z in range(zs):
            if only is None or z in only:
                pairs += [(z * CORES + c, (z ^ m) * CORES + c) for c in range(CORES)]
        return lax.ppermute(block, "dp", pairs)

    def spread_z(block):
        if zs != 4:
            return [[swap_z(block, m)] for m in range(1, zs)]
        near = swap_z(block, 1)
        middle = swap_z(block, 3, (1, 2))
        through = swap_z(near, 3, (1, 2))
        ends = swap_z(middle, 1)
        last = swap_z(through, 1)
        return [[near], [through, ends], [middle, last]]

    sent = local_call(
        functools.partial(send_kernel, experts, zs),
        [shape_of((2, CAP, width))] * experts + [shape_of((experts, CAP, 2 * chip_width))] * zs,
        [ids, probs, tokens, cotangent],
        4 * rows * tok_rows * width,
        [pltpu.VMEM((rows, width), F32)] * 2
        + [pltpu.VMEM(a.shape, a.dtype) for a in (ids, probs, tokens, cotangent)]
        + [pltpu.SemaphoreType.DMA((4,))],
        space=HBM,
        megabytes=SEND_MB,
    )
    (staged,) = local_call(
        stage_kernel,
        [shape_of(weights.shape)],
        [weights],
        0,
        [pltpu.SemaphoreType.DMA((3,))],
        space=HBM,
    )
    blocks = swap_expert(sent[:experts])
    shares = [sent[experts]] + [swap_z(sent[experts + m], m) for m in range(1, zs)]

    unit = 3 * hidden // sum(PARTS)
    ends = [unit * sum(PARTS[:k]) for k in range(PIECES + 1)]
    cuts = list(zip(ends[:-1], ends[1:]))
    steps = [hi - lo for lo, hi in cuts]
    acts = local_call(
        functools.partial(ffn_kernel, experts, cuts),
        [shape_of((rows, step)) for step in steps],
        [staged, *blocks],
        6 * rows * width * hidden,
    )
    spread = [spread_z(block) for block in acts]
    results = local_call(
        functools.partial(output_kernel, experts, cuts),
        [shape_of((2, CAP, width))] * experts,
        [staged, *acts],
        6 * rows * width * hidden,
    )
    messages = local_call(
        functools.partial(regroup_kernel, experts, zs),
        [shape_of((4, CAP, width))] * experts,
        [*results, *shares],
        0,
    )
    back = feats = swap_expert(messages)
    mixed, grad_tokens, gates = local_call(
        functools.partial(combine_kernel, experts),
        [shape_of((tok_rows, width)), shape_of((tok_rows, width)), shape_of(ids.shape, F32)],
        [ids, probs, cotangent, *back],
        8 * rows * tok_rows * width,
    )

    def swap_core(block):
        return lax.ppermute(block, "dp", [(i, i ^ 1) for i in range(groups)])

    part = chip_width // CORES
    grads = None
    for k in range(PIECES):
        cut = (*cuts[k], hidden)
        step = steps[k]
        pieces = [[acts[k]]] + spread[k][:-1]
        counts = tuple(map(len, pieces))
        pieces = [*feats, *[a for piece in pieces for a in piece]]
        farthest = spread[k][-1]
        flops = 2 * rows * chip_width * step
        body = early_grad_kernel if k + 1 < PIECES else last_early_kernel
        body = functools.partial(body, experts, tuple(range(zs - 1)), zs, counts, cut)
        store_scratch = [pltpu.VMEM((part, step), BF16), pltpu.SemaphoreType.DMA((3,))]
        result = [shape_of((3, part, hidden))]
        if k + 1 < PIECES:
            (total,) = local_call(
                body, [shape_of((chip_width, step), F32)], pieces, (zs - 1) * flops
            )
            own, send = local_call(
                functools.partial(late_grad_kernel, experts, (zs - 1,), zs, (len(farthest),), cut),
                [shape_of((part, step), F32), shape_of((part, step))],
                [*feats, total, *farthest],
                flops,
            )
            store = functools.partial(first_store_kernel, cut)
            inputs = [own, swap_core(send)]
        else:
            own, send, feat = local_call(
                body,
                [
                    shape_of((part, step), F32),
                    shape_of((part, step)),
                    shape_of((rows, chip_width)),
                ],
                pieces,
                (zs - 1) * flops,
            )
            got = swap_core(send)
            other = swap_core(feat)
            across = [swap_core(a) for a in farthest]
            store = functools.partial(last_store_kernel, experts, zs, len(farthest), cut)
            inputs = [*feats, own, got, other, *farthest, *across]
        if grads is not None:
            inputs.append(grads)
        (grads,) = local_call(
            store, result, inputs, flops, store_scratch, out=HBM, reuse=grads is not None
        )
    grad_weights = jnp.transpose(grads, (1, 0, 2))[:, None]
    return mixed, grad_tokens, gates.T, grad_weights


def solution(mesh):
    both = P(("dp", "expert"), None)
    return jax.shard_map(
        per_device,
        mesh=mesh,
        in_specs=(both, both, both, both, P(None, "expert", None, None)),
        out_specs=(both, both, both, P("dp", "expert", None, None)),
        check_vma=False,
    )
```

```python
import functools

import jax
import jax.numpy as jnp
from jax import lax
from jax.experimental import pallas as pl
from jax.experimental.pallas import tpu as pltpu
from jax.sharding import PartitionSpec as P

CAP = 24
CORES = 2
PARTS = (10, 8)
PIECES = len(PARTS)
SEND_MB = 24
F32 = jnp.float32
BF16 = jnp.bfloat16
VMEM = pl.BlockSpec(memory_space=pltpu.VMEM)
HBM = pl.BlockSpec(memory_space=pltpu.HBM)
NT = (((1,), (1,)), ((), ()))
TN = (((0,), (0,)), ((), ()))


def shape_of(dims, dtype=BF16):
    return jax.ShapeDtypeStruct(dims, dtype)


def local_call(
    body, outs, args, flops, scratch=(), megabytes=24, space=VMEM, out=VMEM, reuse=False
):
    moved = sum(a.size * a.dtype.itemsize for a in list(args) + list(outs))
    call = pl.pallas_call(
        body,
        out_shape=outs,
        in_specs=[space] * (len(args) - reuse) + [HBM] * reuse,
        out_specs=[out] * len(outs),
        input_output_aliases={len(args) - 1: 0} if reuse else {},
        scratch_shapes=list(scratch),
        compiler_params=pltpu.CompilerParams(vmem_limit_bytes=megabytes << 20),
        cost_estimate=pl.CostEstimate(
            flops=int(flops), bytes_accessed=int(moved), transcendentals=0
        ),
    )
    if space is HBM:
        args = [pltpu.with_memory_space_constraint(a, pltpu.HBM) for a in args]
    return call(*args)


def slot_map(ids, probs, me, experts):
    tokens = ids.shape[1]
    before = (
        lax.broadcasted_iota(jnp.int32, (tokens, tokens), 0)
        < lax.broadcasted_iota(jnp.int32, (tokens, tokens), 1)
    ).astype(BF16)
    named = []
    weight = []
    for m in range(experts):
        hit = ids == jnp.bitwise_xor(me, m)
        named.append(jnp.sum(hit.astype(F32), axis=0, keepdims=True))
        weight.append(jnp.sum(jnp.where(hit, probs, 0.0), axis=0, keepdims=True))
    mask = jnp.concatenate(named, axis=0)
    pos = jnp.dot(mask.astype(BF16), before, preferred_element_type=F32)
    rank = lax.broadcasted_iota(jnp.int32, (CAP, tokens), 0).astype(F32)
    blocks = []
    slot_probs = []
    for m in range(experts):
        hot = jnp.where((rank == pos[m : m + 1]) & (mask[m : m + 1] > 0.5), 1.0, 0.0)
        blocks.append(hot)
        slot_probs.append(jnp.sum(hot * weight[m], axis=1, keepdims=True))
    return jnp.concatenate(blocks, axis=0), jnp.concatenate(slot_probs, axis=0)


def stage_kernel(w_ref, out_ref, sem):
    copies = [
        pltpu.make_async_copy(w_ref.at[j], out_ref.at[j], sem.at[j])
        for j in range(w_ref.shape[0])
    ]
    for copy in copies:
        copy.start()
    for copy in copies:
        copy.wait()


def send_kernel(experts, zs, *refs):
    sources, refs = refs[:4], refs[4:]
    rows_out, feats_out = refs[:experts], refs[experts : experts + zs]
    scratch = refs[experts + zs : experts + zs + 2]
    held, sem = refs[experts + zs + 2 : -1], refs[-1]
    copies = [
        pltpu.make_async_copy(a, b, sem.at[j]) for j, (a, b) in enumerate(zip(sources, held))
    ]
    for copy in copies:
        copy.start()
    ids_ref, probs_ref, tok_ref, cot_ref = held
    for copy in copies[:2]:
        copy.wait()
    me = lax.axis_index("expert")
    dp = lax.axis_index("dp")
    z, c = dp // CORES, dp % CORES
    onehot, slot_probs = slot_map(ids_ref[...], probs_ref[...], me, experts)
    pick = onehot.astype(BF16)
    copies[2].wait()
    x_rows = jnp.dot(pick, tok_ref[...], preferred_element_type=F32)
    copies[3].wait()
    dy_rows = slot_probs * jnp.dot(pick, cot_ref[...], preferred_element_type=F32)
    part = x_rows.shape[1] // (zs * CORES)
    for j, value in enumerate((x_rows, dy_rows)):
        for m in range(experts):
            rows_out[m][j] = value[m * CAP : (m + 1) * CAP].astype(BF16)
        scratch[j][...] = value
        for m in range(zs):
            chip = jnp.bitwise_xor(z, m) * CORES
            for h in range(CORES):
                start = (chip + jnp.bitwise_xor(c, h)) * part
                piece = scratch[j][:, pl.ds(pl.multiple_of(start, part), part)]
                at = (j * CORES + h) * part
                for k in range(experts):
                    feats_out[m][k, :, at : at + part] = piece[
                        k * CAP : (k + 1) * CAP
                    ].astype(BF16)


def stack_rows(blocks):
    return jnp.concatenate([b.astype(F32) for b in blocks], axis=0).astype(BF16)


def put_columns(outs, cuts, lo, value):
    hi = lo + value.shape[1]
    for out, (at, end) in zip(outs, cuts):
        a, b = max(at, lo), min(end, hi)
        if a < b:
            out[:, a - at : b - at] = value[:, a - lo : b - lo]


def get_columns(refs, cuts, lo, hi):
    parts = []
    for ref, (at, end) in zip(refs, cuts):
        a, b = max(at, lo), min(end, hi)
        if a < b:
            parts.append(ref[:, a - at : b - at])
    return parts[0] if len(parts) == 1 else jnp.concatenate(parts, axis=1)


def ffn_kernel(experts, cuts, w_ref, *refs):
    blocks, outs = refs[:experts], refs[experts:]
    hidden = w_ref.shape[2]
    x = stack_rows([b[0] for b in blocks])
    dy = stack_rows([b[1] for b in blocks])
    gate = jnp.dot(x, w_ref[0], preferred_element_type=F32)
    up = jnp.dot(x, w_ref[1], preferred_element_type=F32)
    s = jax.nn.sigmoid(gate)
    put_columns(outs, cuts, 0, (gate * s * up).astype(BF16))
    grad = jnp.dot(dy, w_ref[2], preferred_element_type=F32)
    gate_grad = grad * up * s * (1.0 + gate * (1.0 - s))
    put_columns(outs, cuts, hidden, gate_grad.astype(BF16))
    put_columns(outs, cuts, 2 * hidden, (grad * (gate * s)).astype(BF16))


def output_kernel(experts, cuts, w_ref, *refs):
    acts, outs = refs[: len(cuts)], refs[len(cuts) :]
    hidden = w_ref.shape[2]
    hid, gg, ug = (get_columns(acts, cuts, j * hidden, (j + 1) * hidden) for j in range(3))
    out = lax.dot_general(w_ref[2], hid, NT, preferred_element_type=F32).T
    part = lax.dot_general(w_ref[0], gg, NT, preferred_element_type=F32)
    part += lax.dot_general(w_ref[1], ug, NT, preferred_element_type=F32)
    part = part.T
    for m in range(experts):
        outs[m][0] = out[m * CAP : (m + 1) * CAP].astype(BF16)
        outs[m][1] = part[m * CAP : (m + 1) * CAP].astype(BF16)


def combine_kernel(experts, ids_ref, probs_ref, cot_ref, *refs):
    blocks, (mixed_ref, gtok_ref, gates_ref) = refs[:experts], refs[experts:]
    ids = ids_ref[...]
    me = lax.axis_index("expert")
    onehot, slot_probs = slot_map(ids, probs_ref[...], me, experts)
    pick = onehot.astype(BF16)
    out = jnp.concatenate([b[0].astype(F32) for b in blocks], axis=0)
    weighted = out * slot_probs
    high = weighted.astype(BF16)
    low = (weighted - high.astype(F32)).astype(BF16)
    mixed = lax.dot_general(pick, high, TN, preferred_element_type=F32)
    mixed += lax.dot_general(pick, low, TN, preferred_element_type=F32)
    mixed_ref[...] = mixed.astype(BF16)
    part = stack_rows([b[1] for b in blocks])
    gtok = lax.dot_general(pick, part, TN, preferred_element_type=F32)
    gtok_ref[...] = gtok.astype(BF16)
    cot_rows = jnp.dot(pick, cot_ref[...], preferred_element_type=F32)
    inner = jnp.sum(out * cot_rows, axis=1, keepdims=True)
    spread = onehot * inner
    gates = jnp.zeros(ids.shape, F32)
    for m in range(experts):
        value = jnp.sum(spread[m * CAP : (m + 1) * CAP], axis=0, keepdims=True)
        gates = jnp.where(ids == jnp.bitwise_xor(me, m), value, gates)
    gates_ref[...] = gates


def regroup_kernel(experts, zs, *refs):
    results, shares, outs = refs[:experts], refs[experts : experts + zs], refs[experts + zs :]
    wide = shares[0].shape[2]
    for k in range(experts):
        outs[k][:2] = results[k][...]
        for m in range(zs):
            row, at = divmod(m * wide, results[k].shape[2])
            outs[k][2 + row, :, at : at + wide] = shares[m][k]


def features_of(message, chip, zs):
    wide = 2 * message.shape[2] // zs
    row, at = divmod(chip * wide, message.shape[2])
    return message[2 + row, :, at : at + wide]


def pick_rows(refs):
    value = refs[0][...]
    for more in refs[1:]:
        value += more[...]
    return value


def contract(rows_f, rows_a, cut):
    lo, hi, hidden = cut
    half = rows_f.shape[1] // 2
    sums = []
    split = min(max(hidden - lo, 0), hi - lo)
    if split > 0:
        sums.append(
            lax.dot_general(rows_f[:, half:], rows_a[:, :split], TN, preferred_element_type=F32)
        )
    if split < hi - lo:
        sums.append(
            lax.dot_general(rows_f[:, :half], rows_a[:, split:], TN, preferred_element_type=F32)
        )
    return sums[0] if len(sums) == 1 else jnp.concatenate(sums, axis=1)


def grad_sums(feats, chips, zs, picks, refs, cut):
    rows_f = stack_rows([features_of(f, m, zs) for m in chips for f in feats])
    acts = []
    for n in picks:
        acts.append(pick_rows(refs[:n]))
        refs = refs[n:]
    rows_a = acts[0] if len(acts) == 1 else jnp.concatenate(acts, axis=0)
    return contract(rows_f, rows_a, cut)


def early_grad_kernel(experts, chips, zs, picks, cut, *refs):
    feats, acts, total = refs[:experts], refs[experts:-1], refs[-1]
    total[...] = grad_sums(feats, chips, zs, picks, acts, cut)


def late_grad_kernel(experts, chips, zs, picks, cut, *refs):
    feats, (total, *acts), (own, send) = refs[:experts], refs[experts:-2], refs[-2:]
    more = grad_sums(feats, chips, zs, picks, acts, cut)
    half = more.shape[0] // CORES
    own[...] = total[:half] + more[:half]
    send[...] = (total[half:] + more[half:]).astype(BF16)


def last_early_kernel(experts, chips, zs, picks, cut, *refs):
    feats, acts, (own, send, feat) = refs[:experts], refs[experts:-3], refs[-3:]
    total = grad_sums(feats, chips, zs, picks, acts, cut)
    half = total.shape[0] // CORES
    own[...] = total[:half]
    send[...] = total[half:].astype(BF16)
    rows_f = stack_rows([features_of(f, zs - 1, zs) for f in feats])
    part = rows_f.shape[1] // 4
    feat[:, :part] = rows_f[:, part : 2 * part]
    feat[:, part:] = rows_f[:, 3 * part :]


def store_piece(value, cut, held, out, sem):
    lo, hi, hidden = cut
    held[...] = value.astype(BF16)
    copies = []
    for j in range(3):
        a, b = max(lo, j * hidden), min(hi, (j + 1) * hidden)
        if a < b:
            source = held.at[:, a - lo : b - lo]
            target = out.at[(j + 2) % 3, :, a - j * hidden : b - j * hidden]
            copies.append(pltpu.make_async_copy(source, target, sem.at[j]))
    for copy in copies:
        copy.start()
    for copy in copies:
        copy.wait()


def first_store_kernel(cut, own, got, *refs):
    out, held, sem = refs[-3:]
    store_piece(own[...] + got[...].astype(F32), cut, held, out, sem)


def last_store_kernel(experts, zs, picks, cut, *refs):
    feats, (own, got, other_feat) = refs[:experts], refs[experts : experts + 3]
    acts = refs[experts + 3 : experts + 3 + 2 * picks]
    _, out, held, sem = refs[experts + 3 + 2 * picks :]
    rows_f = stack_rows([features_of(f, zs - 1, zs) for f in feats])
    part = rows_f.shape[1] // 4
    mine = jnp.concatenate([rows_f[:, :part], rows_f[:, 2 * part : 3 * part]], axis=1)
    rows_f = jnp.concatenate([mine, other_feat[...]], axis=0)
    rows_a = jnp.concatenate([pick_rows(acts[:picks]), pick_rows(acts[picks:])], axis=0)
    total = own[...] + got[...].astype(F32) + contract(rows_f, rows_a, cut)
    store_piece(total, cut, held, out, sem)


def per_device(tokens, expert_ids, gate_probs, cotangent, expert_weights):
    tok_rows, width = tokens.shape
    experts = lax.axis_size("expert")
    groups = lax.axis_size("dp")
    zs = groups // CORES
    hidden = expert_weights.shape[3]
    rows = experts * CAP
    chip_width = width // zs
    weights = jnp.transpose(expert_weights[:, 0], (1, 0, 2))
    ids, probs = expert_ids.T, gate_probs.T

    def swap_expert(blocks):
        moved = list(blocks)
        for m in range(experts - 1, 0, -1):
            pairs = [(i, i ^ m) for i in range(experts)]
            moved[m] = lax.ppermute(blocks[m], "expert", pairs)
        return moved

    def swap_z(block, m, only=None):
        pairs = []
        for z in range(zs):
            if only is None or z in only:
                pairs += [(z * CORES + c, (z ^ m) * CORES + c) for c in range(CORES)]
        return lax.ppermute(block, "dp", pairs)

    def spread_z(block):
        if zs != 4:
            return [[swap_z(block, m)] for m in range(1, zs)]
        near = swap_z(block, 1)
        middle = swap_z(block, 3, (1, 2))
        through = swap_z(near, 3, (1, 2))
        ends = swap_z(middle, 1)
        last = swap_z(through, 1)
        return [[near], [through, ends], [middle, last]]

    sent = local_call(
        functools.partial(send_kernel, experts, zs),
        [shape_of((2, CAP, width))] * experts + [shape_of((experts, CAP, 2 * chip_width))] * zs,
        [ids, probs, tokens, cotangent],
        4 * rows * tok_rows * width,
        [pltpu.VMEM((rows, width), F32)] * 2
        + [pltpu.VMEM(a.shape, a.dtype) for a in (ids, probs, tokens, cotangent)]
        + [pltpu.SemaphoreType.DMA((4,))],
        space=HBM,
        megabytes=SEND_MB,
    )
    (staged,) = local_call(
        stage_kernel,
        [shape_of(weights.shape)],
        [weights],
        0,
        [pltpu.SemaphoreType.DMA((3,))],
        space=HBM,
    )
    blocks = swap_expert(sent[:experts])
    shares = [sent[experts]] + [swap_z(sent[experts + m], m) for m in range(1, zs)]

    unit = 3 * hidden // sum(PARTS)
    ends = [unit * sum(PARTS[:k]) for k in range(PIECES + 1)]
    cuts = list(zip(ends[:-1], ends[1:]))
    steps = [hi - lo for lo, hi in cuts]
    acts = local_call(
        functools.partial(ffn_kernel, experts, cuts),
        [shape_of((rows, step)) for step in steps],
        [staged, *blocks],
        6 * rows * width * hidden,
    )
    spread = [spread_z(block) for block in acts]
    results = local_call(
        functools.partial(output_kernel, experts, cuts),
        [shape_of((2, CAP, width))] * experts,
        [staged, *acts],
        6 * rows * width * hidden,
    )
    messages = local_call(
        functools.partial(regroup_kernel, experts, zs),
        [shape_of((4, CAP, width))] * experts,
        [*results, *shares],
        0,
    )
    back = feats = swap_expert(messages)
    mixed, grad_tokens, gates = local_call(
        functools.partial(combine_kernel, experts),
        [shape_of((tok_rows, width)), shape_of((tok_rows, width)), shape_of(ids.shape, F32)],
        [ids, probs, cotangent, *back],
        8 * rows * tok_rows * width,
    )

    def swap_core(block):
        return lax.ppermute(block, "dp", [(i, i ^ 1) for i in range(groups)])

    part = chip_width // CORES
    grads = None
    for k in range(PIECES):
        cut = (*cuts[k], hidden)
        step = steps[k]
        pieces = [[acts[k]]] + spread[k][:-1]
        counts = tuple(map(len, pieces))
        pieces = [*feats, *[a for piece in pieces for a in piece]]
        farthest = spread[k][-1]
        flops = 2 * rows * chip_width * step
        body = early_grad_kernel if k + 1 < PIECES else last_early_kernel
        body = functools.partial(body, experts, tuple(range(zs - 1)), zs, counts, cut)
        store_scratch = [pltpu.VMEM((part, step), BF16), pltpu.SemaphoreType.DMA((3,))]
        result = [shape_of((3, part, hidden))]
        if k + 1 < PIECES:
            (total,) = local_call(
                body, [shape_of((chip_width, step), F32)], pieces, (zs - 1) * flops
            )
            own, send = local_call(
                functools.partial(late_grad_kernel, experts, (zs - 1,), zs, (len(farthest),), cut),
                [shape_of((part, step), F32), shape_of((part, step))],
                [*feats, total, *farthest],
                flops,
            )
            store = functools.partial(first_store_kernel, cut)
            inputs = [own, swap_core(send)]
        else:
            own, send, feat = local_call(
                body,
                [
                    shape_of((part, step), F32),
                    shape_of((part, step)),
                    shape_of((rows, chip_width)),
                ],
                pieces,
                (zs - 1) * flops,
            )
            got = swap_core(send)
            other = swap_core(feat)
            across = [swap_core(a) for a in farthest]
            store = functools.partial(last_store_kernel, experts, zs, len(farthest), cut)
            inputs = [*feats, own, got, other, *farthest, *across]
        if grads is not None:
            inputs.append(grads)
        (grads,) = local_call(
            store, result, inputs, flops, store_scratch, out=HBM, reuse=grads is not None
        )
    grad_weights = jnp.transpose(grads, (1, 0, 2))[:, None]
    return mixed, grad_tokens, gates.T, grad_weights


def solution(mesh):
    both = P(("dp", "expert"), None)
    return jax.shard_map(
        per_device,
        mesh=mesh,
        in_specs=(both, both, both, both, P(None, "expert", None, None)),
        out_specs=(both, both, both, P("dp", "expert", None, None)),
        check_vma=False,
    )
```
